512 devices in a mesh: leaf: 128 (over z, x, core), obs: 4 (over y).
Axes of the slice: x: 4, y: 4, z: 16, core: 2. Of those that a mesh axis runs over, the one named last changes fastest.
Arguments:
- samples_z: bfloat16 [64, 32768], P('obs', 'leaf'), may hold values from -6 to 6
- diag_block: bfloat16 [32768, 256], P('leaf'), as said below
- level_basis: bfloat16 [7, 64, 32768], P(None, None, 'leaf'), may hold values from -6 to 6
- site_xy: float32 [2, 32768], P(None, 'leaf'), may hold values from 0 to 1, as said below
- obs_site: int32 [16384], P('leaf'), may hold values from 0 to 255
- obs_value: float32 [16384], P('leaf'), may hold values from -6 to 6
- obs_count: int32 [128], P('leaf'), may hold values from 1 to 128, 8192 in all
- inverse_rows: float32 [8192, 8192], P(('leaf', 'obs')), may hold values from -0.001953125 to 0.001953125
Outputs:
- conditional: float32 [64, 32768], P('obs', 'leaf')
The draws below stay inside these ranges and needn't reach their ends.
Inputs may be any that keep to these rules, and one draw needn't show every extreme that they name: `obs_count`: each leaf block's count of observations; the counts sum to 8192 and the largest is exactly 128. `obs_site`: slots at or past a block's count are not used. `diag_block`: each leaf block is symmetric. `site_xy`: coordinates lie in the unit square; the sites of each leaf block lie in one cell of a recursive halving of the square that follows the tree of blocks.
All inputs are finite; a program needn't handle non-finite values.
Results may differ from the reference program's by a relative error of at most 0.0003.
Values sent between devices are 32-bit elements; how exact they have to be, the bound alone decides.
No kernel may reach another device: no remote copies, remote signals or barrier semaphores. Data moves between devices by JAX's collectives and lax.ppermute only.
A program may use at most 64 MiB of HBM per device.

```python
import math
import jax
import jax.numpy as jnp
import numpy as np
from jax import lax

NB = 256
S = 64
R = 64
OCAP = 128
LEVELS = 7
NSITES = 32768
M = 8192
SLOTS = 16384
N_LEAF = 128


def draw_site_xy(key, part):
    index = jnp.arange(NSITES, dtype=jnp.int32)
    block = index // NB
    column = jnp.zeros((NSITES,), jnp.int32)
    row = jnp.zeros((NSITES,), jnp.int32)
    for level in range(LEVELS):
        digit = block >> level & 1
        if level % 2 == 0:
            column = column + (digit << level // 2)
        else:
            row = row + (digit << level // 2)
    columns = 2 ** ((LEVELS + 1) // 2)
    rows = 2 ** (LEVELS // 2)
    jitter = jax.random.uniform(key, (2, NSITES), jnp.float32)
    coord_x = (column.astype(jnp.float32) + jitter[0]) / columns
    coord_y = (row.astype(jnp.float32) + jitter[1]) / rows
    return jnp.stack([coord_x, coord_y], axis=0).astype(jnp.float32)


def draw_diag_block(key, part):
    raw = jax.random.normal(key, (N_LEAF, NB, NB), jnp.float32)
    paired = (raw + jnp.swapaxes(raw, 1, 2)) * (1.0 / jnp.sqrt(jnp.float32(2 * NB)))
    return paired.reshape(N_LEAF * NB, NB).astype(jnp.bfloat16)


def place_ends(values, rng, low, top_value):
    dims = values.shape
    place = [jax.random.randint(jax.random.fold_in(rng, axis), (), 0, dims[axis]) for axis in range(len(dims))]
    values = values.at[tuple(place)].set(low)
    longest = dims.index(max(dims))
    place[longest] = (place[longest] + 1) % dims[longest]
    return values.at[tuple(place)].set(top_value)


def steps_of(rng, extent, split, smallest, high):
    gain, own = 1.0, jax.random.fold_in(rng, 6)
    for axis_at, shards_of in split:
        steps = jnp.exp(jax.random.uniform(jax.random.fold_in(own, axis_at), (shards_of,), jnp.float32, smallest / len(split), high / len(split)))
        gain = gain * jnp.repeat(steps, extent[axis_at] // shards_of).reshape([-1 if axis == axis_at else 1 for axis in range(len(extent))])
    return gain


def profile(amount, total, reach, slope):
    portions = [(1 << 20) // math.isqrt(rank ** slope) + 1 for rank in range(2, amount + 1)]
    spare, given = total - reach - (amount - 1), [1] * (amount - 1)
    while spare > 0:
        candidates = [i for i in range(amount - 1) if given[i] < reach]
        whole, left = sum([portions[i] for i in candidates]), spare
        for i in candidates:
            more = min(reach - given[i], max(1, left * portions[i] // whole), spare)
            given[i] = given[i] + more
            spare = spare - more
    return np.array([reach] + given)


def ragged(key, amount, total, most, skew):
    if amount == 2:
        one = jax.random.randint(key, (), max(1, total - most), min(most, total - 1) + 1)
        return jnp.stack([one, total - one])
    sizes = jnp.asarray(profile(amount, total, most, skew), jnp.int32)
    pairs = (amount - 1) // 2
    source_of, taker = sizes[1:1 + 2 * pairs:2], sizes[2:2 + 2 * pairs:2]
    margin = jnp.minimum(source_of - 1, most - taker)
    moved = jax.random.randint(jax.random.fold_in(key, 1), (pairs,), 0, 1 << 20) % (margin + 1)
    sizes = sizes.at[1:1 + 2 * pairs:2].set(source_of - moved).at[2:2 + 2 * pairs:2].set(taker + moved)
    return sizes[jax.random.permutation(jax.random.fold_in(key, 2), amount)]


def gaussian(own_key, extent, scale, most, pieces=(), held_as=jnp.bfloat16):
    factor_of = steps_of(own_key, extent, pieces, -0.22, 0.18) if pieces else 1.0
    result = jax.random.normal(own_key, extent, jnp.float32) * scale * factor_of
    return jnp.minimum(jnp.maximum(result, -most), most).astype(held_as)


def setup_inputs(seed: int = 0) -> dict:
    keys = jax.random.split(jax.random.key(seed), 9)
    return {
        "samples_z": gaussian(keys[0], (S, NSITES), 1.0, 6.0, ((0, 4), (1, 128))),
        "diag_block": draw_diag_block(jax.random.fold_in(keys[8], 71), 0),
        "level_basis": gaussian(keys[2], (LEVELS, R, NSITES), 1.0, 6.0, ((2, 128),)),
        "site_xy": draw_site_xy(jax.random.fold_in(keys[8], 71), 0),
        "obs_site": place_ends(jax.random.randint(keys[4], (SLOTS,), 0, NB), jax.random.fold_in(keys[4], 1), 0, NB - 1).astype(jnp.int32),
        "obs_value": gaussian(keys[5], (SLOTS,), 1.0, 6.0, ((0, 128),), jnp.float32),
        "obs_count": ragged(keys[6], N_LEAF, M, OCAP, 2).astype(jnp.int32),
        "inverse_rows": gaussian(keys[7], (M, M), (M * 1024) ** -0.5, 0.001953125, ((0, 512),), jnp.float32),
    }


corr_length = 0.15

def compact_index(counts, slot_count, total):
    inclusive = jnp.cumsum(counts).astype(jnp.int32)
    number = jnp.arange(total, dtype=jnp.int32)
    passed = (inclusive[None, :] <= number[:, None]).astype(jnp.int32)
    owner = lax.optimization_barrier(jnp.sum(passed, axis=1)).astype(jnp.int32)
    base = lax.optimization_barrier(jnp.sum(passed * counts[None, :], axis=1)).astype(jnp.int32)
    return (owner * slot_count + number - base).astype(jnp.int32)

def kernel_tile(obs_xy, block_xy):
    delta_x = obs_xy[0][:, None] - block_xy[0][None, :]
    delta_y = obs_xy[1][:, None] - block_xy[1][None, :]
    distance = jnp.sqrt(delta_x * delta_x + delta_y * delta_y)
    return jnp.exp(-distance / corr_length)

def reference(samples_z, diag_block, level_basis, site_xy, obs_site, obs_value, obs_count, inverse_rows):
    draws = samples_z.astype(jnp.float32).reshape(S, N_LEAF, NB)
    blocks = diag_block.astype(jnp.float32).reshape(N_LEAF, NB, NB)
    field_diag = jnp.einsum('spn,pnm->spm', draws, blocks, precision=lax.Precision.HIGHEST)
    basis = level_basis.astype(jnp.float32).reshape(LEVELS, R, N_LEAF, NB)
    project = jnp.einsum('spn,lrpn->pslr', draws, basis, precision=lax.Precision.HIGHEST)
    coef_list = []
    for level in range(LEVELS):
        width = 2 ** level
        grouped = project[:, :, level, :].reshape(N_LEAF // (2 * width), 2, width, S, R)
        sums = lax.optimization_barrier(jnp.sum(grouped, axis=2))
        sibling = sums[:, ::-1]
        spread = jnp.broadcast_to(sibling[:, :, None], (N_LEAF // (2 * width), 2, width, S, R)).reshape(N_LEAF, S, R)
        factor = 0.5 / jnp.sqrt(jnp.float32(R * width * NB))
        coef_list.append(spread * factor)
    coefficients = jnp.stack(coef_list, axis=2)
    field_low = jnp.einsum('pslr,lrpn->spn', coefficients, basis, precision=lax.Precision.HIGHEST)
    field = (field_diag + field_low).reshape(S, NSITES)
    obs_index = compact_index(obs_count, OCAP, M)
    owner = (obs_index // OCAP).astype(jnp.int32)
    global_site = (owner * NB + obs_site[obs_index]).astype(jnp.int32)
    residual = obs_value[obs_index][None, :] - field[:, global_site]
    coef = lax.dot_general(residual, inverse_rows, (((1,), (1,)), ((), ())), precision=lax.Precision.HIGHEST, preferred_element_type=jnp.float32)
    obs_xy = site_xy[:, global_site]
    block_xy = site_xy.reshape(2, N_LEAF, NB).transpose(1, 0, 2)

    def one_block(xy_block):
        tile = kernel_tile(obs_xy, xy_block)
        return jnp.dot(coef, tile, precision=lax.Precision.HIGHEST, preferred_element_type=jnp.float32)
    correction = lax.map(one_block, block_xy)
    correction = correction.transpose(1, 0, 2).reshape(S, NSITES)
    return field + correction
```

```python
import math

import jax
import jax.numpy as jnp
from jax import lax
from jax.experimental import pallas as pl
from jax.experimental.pallas import tpu as pltpu
from jax.sharding import Mesh, PartitionSpec as P


corr_length = 0.15
SCALE = math.log2(math.e) / corr_length
LEVELS = 7
R = 64
XC = 8
NZ = 16
S = 16
NB = 256
CAP = 128
M = 8192
ROWS = 64
F32 = jnp.float32
BF16 = jnp.bfloat16

VMEM = pl.BlockSpec(memory_space=pltpu.VMEM)
HBM = pl.BlockSpec(memory_space=pltpu.MemorySpace.HBM)
SMEM = pl.BlockSpec(memory_space=pltpu.SMEM)
NT = (((1,), (1,)), ((), ()))

VMEM_MIB = {'local': 2, 'observed': 1, 'near': 2, 'field': 4, 'inverse': 8, 'spread': 4, 'coef': 10, 'cross': 60, 'pair': 4, 'final': 14}


def dot(a, b, dims=(((1,), (0,)), ((), ()))):
    return lax.dot_general(a, b, dims, preferred_element_type=F32)


def split2(v):
    hi = v.astype(BF16)
    return hi, (v - hi.astype(F32)).astype(BF16)


def split3(v):
    hi = v.astype(BF16)
    rest = v - hi.astype(F32)
    mid = rest.astype(BF16)
    return hi, mid, (rest - mid.astype(F32)).astype(BF16)


def fetch(sems, pairs):
    copies = [pltpu.make_async_copy(src, dst, sems.at[i]) for i, (src, dst) in enumerate(pairs)]
    for copy in copies:
        copy.start()
    for copy in copies:
        copy.wait()


def project_kernel(z_ref, basis_ref, count_ref, out_ref):
    proj = dot(z_ref[...], basis_ref[...], NT)
    count = jnp.full((S, R), count_ref[0], jnp.int32).astype(F32)
    piece = jnp.concatenate([proj, count], axis=1)
    for q in range(XC):
        out_ref[q] = piece


def observed_kernel(value_hbm, value_ref, sems):
    fetch(sems, [(value_hbm, value_ref)])


def local_kernel(
    z_ref, diag_hbm, xy_hbm, site_hbm, basis_hbm, field_ref, pick_ref, xy_at_ref, xy_ref, basis_ref, diag_ref, site_ref, sems
):
    fetch(sems, [(diag_hbm, diag_ref), (xy_hbm, xy_ref), (site_hbm, site_ref), (basis_hbm, basis_ref)])
    field_ref[...] = dot(z_ref[...], diag_ref[...])
    site = lax.broadcasted_iota(jnp.int32, (NB, CAP), 0)
    pick = jnp.where(site == site_ref[...], 1.0, 0.0).astype(BF16)
    pick_ref[...] = pick
    known = jnp.concatenate([xy_ref[...] * SCALE, jnp.zeros((6, NB), F32)], axis=0)
    at = dot(jnp.concatenate(split3(known), axis=0), pick)
    at = (at[16:] + at[8:16]) + at[:8]
    half = [at[:2, :R], at[:2, R:]]
    xy_at_ref[...] = jnp.concatenate([half[0][0:1], half[1][0:1], half[0][1:2], half[1][1:2], jnp.zeros((12, R), F32)], axis=0)


def near_kernel(recv_ref, xy_at_ref, near_ref, out_ref):
    me = lax.axis_index("x") * 2 + lax.axis_index("core")
    my_z = lax.axis_index("z")
    level = lax.broadcasted_iota(jnp.int32, (S, 512), 1) // R
    row = lax.broadcasted_iota(jnp.int32, (S, R), 0)
    total = jnp.zeros((S, 512), F32)
    extra = xy_at_ref[...]
    for q in range(XC):
        apart = me ^ q
        own_level = jnp.where(apart == 1, 0, jnp.where(apart < 4, 1, 2))
        own_level = jnp.where(apart == 0, -1, own_level)
        got = recv_ref[q]
        total = total + jnp.where((level == own_level) | (level >= 3), got, 0.0)
        extra = jnp.where(row == q + 8, got[:, LEVELS * R :], extra)
    near_ref[...] = total
    parts = [jnp.concatenate([total[:, (3 + k) * R : (4 + k) * R], extra], axis=1) for k in range(4)]
    for z in range(NZ):
        apart = my_z ^ z
        out_ref[z] = jnp.where(apart >= 8, parts[3], jnp.where(apart >= 4, parts[2], jnp.where(apart >= 2, parts[1], parts[0])))


def field_kernel(recv_ref, near_ref, local_ref, basis_ref, pick_ref, value_ref, field_ref, out_ref):
    my_z = lax.axis_index("z")
    far = [jnp.zeros((S, CAP), F32) for _ in range(4)]
    for z in range(NZ):
        apart = my_z ^ z
        got = recv_ref[z]
        for k in range(4):
            mine = (apart >= 2**k) & (apart < 2 ** (k + 1))
            far[k] = far[k] + jnp.where(mine, got, 0.0)
    coef = jnp.concatenate([near_ref[:, : 3 * R]] + [f[:, :R] for f in far], axis=1)
    level = lax.broadcasted_iota(jnp.int32, (S, LEVELS * R), 1) // R
    factor = jnp.zeros((S, LEVELS * R), F32)
    for k in range(LEVELS):
        factor = jnp.where(level == k, 0.5 / math.sqrt(R * NB * 2.0**k), factor)
    coef = coef * factor
    low = dot(jnp.concatenate(split3(coef), axis=0), basis_ref[...])
    field = local_ref[...] + ((low[2 * S :] + low[S : 2 * S]) + low[:S])
    field_ref[...] = field
    at = dot(jnp.concatenate(split3(field), axis=0), pick_ref[...])
    residual = value_ref[...] - ((at[2 * S :] + at[S : 2 * S]) + at[:S])
    for z in range(NZ):
        out_ref[z] = residual


def spread_kernel(recv_ref, extra_ref, out_ref):
    for x in range(4):
        for z in range(NZ):
            out_ref[x, S * z : S * (z + 1)] = recv_ref[z]
    for z in range(0, NZ, 4):
        rows = []
        for zz in range(z, z + 4):
            rows += [jnp.concatenate([extra_ref[zz, 2 * i : 2 * i + 1, R:], extra_ref[zz, 2 * i + 1 : 2 * i + 2, R:]], axis=1) for i in range(2)]
        rows = jnp.concatenate(rows, axis=0)
        for x in range(4):
            out_ref[x, S * NZ + 2 * z : S * NZ + 2 * z + 8] = rows


def inverse_kernel(*refs):
    *blocks, out_ref = refs
    my_y = lax.axis_index("y")

    def one_part(j, carry):
        at = pl.multiple_of(j * 256, 256)
        got = [ref[:, pl.ds(at, 256)] for ref in blocks]
        rows = []
        for y in range(4):
            apart = my_y ^ y
            rows.append(jnp.where(apart >= 2, jnp.where(apart == 2, got[2], got[3]), jnp.where(apart == 0, got[0], got[1])))
        rows = jnp.concatenate(rows, axis=0)
        hi = rows.astype(BF16).astype(F32)
        out_ref[pl.ds(at, 256)] = jnp.transpose(jnp.concatenate([hi, rows - hi], axis=0)).astype(BF16)
        return carry

    lax.fori_loop(0, M // 256, one_part, 0, unroll=4)


def coef_kernel(base_ref, count_ref, own_ref, other_ref, inv_ref, out_ref, xy_ref, packed):
    core = lax.axis_index("core")
    lane = lax.broadcasted_iota(jnp.int32, (S, CAP), 1)

    def one_column(x, carry):
        for ref, c in ((own_ref, core), (other_ref, 1 - core)):
            for z in range(NZ):
                p = 8 * z + 2 * x + c
                base, count = base_ref[p], count_ref[p]
                shift = base % CAP
                start = pl.multiple_of(base - shift, CAP)
                end = shift + count
                first = (lane >= shift) & (lane < end)
                second = lane < end - CAP
                got = pltpu.roll(ref[x, S * z : S * (z + 1)], shift, 1)
                pltpu.store(packed.at[:, pl.ds(start, CAP)], got, mask=first)
                pltpu.store(packed.at[:, pl.ds(start + CAP, CAP)], got, mask=second)
                got = pltpu.roll(ref[x, S * NZ + 2 * z : S * NZ + 2 * z + 2], shift, 1)
                pltpu.store(xy_ref.at[:, pl.ds(start, CAP)], got, mask=first[:2])
                pltpu.store(xy_ref.at[:, pl.ds(start + CAP, CAP)], got, mask=second[:2])
        return carry

    lax.fori_loop(0, 4, one_column, 0)
    acc = jnp.zeros((2 * S, 2 * ROWS), F32)
    width = 1024
    for k in range(0, M, width):
        acc = acc + dot(jnp.concatenate(split2(packed[:, k : k + width]), axis=0), inv_ref[k : k + width])
    coef = acc[:S] + acc[S:]
    piece = jnp.concatenate([coef[:, :ROWS] + coef[:, ROWS:], jnp.zeros((S, CAP - ROWS), F32)], axis=1)
    for z in range(NZ):
        out_ref[z] = piece


def pair_kernel(recv_ref, out_ref):
    for k in range(NZ // 2):
        pair = jnp.concatenate([recv_ref[2 * k][:, :ROWS], recv_ref[2 * k + 1][:, :ROWS]], axis=1)
        for q in range(XC):
            out_ref[q, k] = pair


CHUNK = 512


def cross_kernel(obs_ref, xy_ref, out_hbm, buf, sems):
    sx = xy_ref[0:1] * SCALE
    sy = xy_ref[1:2] * SCALE

    def copy(i, slot):
        return pltpu.make_async_copy(buf.at[slot], out_hbm.at[pl.ds(pl.multiple_of(i * CHUNK, CHUNK), CHUNK)], sems.at[slot])

    def two_chunks(j, carry):
        for slot in range(2):
            i = 2 * j + slot

            @pl.when(j > 0)
            def _():
                copy(i - 2, slot).wait()

            for row in range(0, CHUNK, CAP):
                at = pl.multiple_of(i * CHUNK + row, CAP)
                ox = jnp.transpose(jnp.broadcast_to(obs_ref[0:1, pl.ds(at, CAP)], (CAP, CAP)))
                oy = jnp.transpose(jnp.broadcast_to(obs_ref[1:2, pl.ds(at, CAP)], (CAP, CAP)))
                for h in range(0, NB, CAP):
                    dx = ox - sx[:, h : h + CAP]
                    dy = oy - sy[:, h : h + CAP]
                    square = jnp.maximum(dx * dx + dy * dy, 1e-30)
                    hi, lo = split2(jnp.exp2(-(square * lax.rsqrt(square))))
                    buf[slot, row : row + CAP, h : h + CAP] = hi
                    buf[slot, row : row + CAP, NB + h : NB + h + CAP] = lo
            copy(i, slot).start()
        return carry

    steps = M // CHUNK
    lax.fori_loop(0, steps // 2, two_chunks, 0)
    for slot in range(2):
        copy(steps - 2 + slot, slot).wait()


def final_kernel(recv_ref, tile_ref, field_ref, out_ref):
    lane = lax.broadcasted_iota(jnp.int32, (S, CAP), 1)
    acc = jnp.zeros((2 * S, 2 * NB), F32)
    for k in range(NZ // 2):
        first, second = [], []
        for x in range(XC // 2):
            even, odd = recv_ref[2 * x, k], recv_ref[2 * x + 1, k]
            first.append(jnp.where(lane < ROWS, even, pltpu.roll(odd, ROWS, 1)))
            second.append(jnp.where(lane < ROWS, pltpu.roll(even, ROWS, 1), odd))
        left = jnp.concatenate(split2(jnp.concatenate(first + second, axis=1)), axis=0)
        acc = acc + dot(left, tile_ref[1024 * k : 1024 * (k + 1)])
    acc = acc[:S] + acc[S:]
    out_ref[...] = field_ref[...] + (acc[:, :NB] + acc[:, NB:])


def call(name, kernel, out, specs, scratch=(), flops=0, nbytes=0, out_specs=None):
    shapes = [jax.ShapeDtypeStruct(s, d) for s, d in out]
    return pl.pallas_call(
        kernel,
        out_shape=shapes,
        in_specs=specs,
        out_specs=out_specs or [VMEM] * len(shapes),
        scratch_shapes=list(scratch),
        compiler_params=pltpu.CompilerParams(vmem_limit_bytes=VMEM_MIB[name] << 20 if name in VMEM_MIB else None),
        cost_estimate=pl.CostEstimate(flops=flops, bytes_accessed=nbytes, transcendentals=0),
    )


def exchange(piece, axes):
    return lax.all_to_all(piece, axes, 0, 0, tiled=True)


def body(samples_z, diag_block, level_basis, site_xy, obs_site, obs_value, obs_count, inverse_rows):
    basis = level_basis.reshape(LEVELS * R, NB)
    blocks = [inverse_rows]
    for d in (1, 2, 3):
        blocks.append(lax.ppermute(inverse_rows, "y", [(y, y ^ d) for y in range(4)]))

    (piece,) = call("project", project_kernel, [((XC, S, 512), F32)], [VMEM, VMEM, SMEM])(samples_z, basis, obs_count)
    recv = exchange(piece, ("x", "core"))
    local, pick, xy_at, xy, basis = call(
        "local",
        local_kernel,
        [((S, NB), F32), ((NB, CAP), BF16), ((S, R), F32), ((2, NB), F32), ((LEVELS * R, NB), BF16)],
        [VMEM] + [HBM] * 4,
        [pltpu.VMEM((NB, NB), BF16), pltpu.VMEM((1, CAP), jnp.int32), pltpu.SemaphoreType.DMA((4,))],
        flops=2 * S * NB * NB,
        nbytes=1 << 18,
    )(samples_z, diag_block, site_xy, obs_site.reshape(1, CAP), basis)
    (value,) = call("observed", observed_kernel, [((1, CAP), F32)], [HBM], [pltpu.SemaphoreType.DMA((1,))])(obs_value.reshape(1, CAP))
    near, piece = call("near", near_kernel, [((S, 512), F32), ((NZ, S, CAP), F32)], [VMEM] * 2)(recv, xy_at)
    extra = exchange(piece, "z")
    counts = extra[:, 8:, R].reshape(XC * NZ)
    order = jnp.arange(XC * NZ, dtype=jnp.int32)
    base = jnp.sum(jnp.where(order[None, :] < order[:, None], counts[None, :], 0.0), axis=1).astype(jnp.int32)
    counts = counts.astype(jnp.int32)
    field, piece = call("field", field_kernel, [((S, NB), F32), ((NZ, S, CAP), F32)], [VMEM] * 6)(
        extra, near, local, basis, pick, value
    )
    (inv,) = call(
        "inverse", inverse_kernel, [((M, 2 * ROWS), BF16)], [VMEM] * 4, flops=20 * ROWS * M, nbytes=8 * ROWS * M
    )(*blocks)
    recv = exchange(piece, "z")
    (piece,) = call("spread", spread_kernel, [((4, 18 * NZ, CAP), F32)], [VMEM] * 2)(recv, extra)
    own = exchange(piece, "x")
    other = lax.ppermute(own, "core", [(0, 1), (1, 0)])
    piece, obs_xy = call(
        "coef",
        coef_kernel,
        [((NZ, S, CAP), F32), ((2, M + 2 * CAP), F32)],
        [SMEM, SMEM, VMEM, VMEM, VMEM],
        [pltpu.VMEM((S, M + 2 * CAP), F32)],
        flops=4 * 2 * S * ROWS * M,
        nbytes=4 * ROWS * M,
    )(base, counts, own, other, inv)
    (tile,) = call(
        "cross",
        cross_kernel,
        [((M, 2 * NB), BF16)],
        [VMEM, VMEM],
        [pltpu.VMEM((2, CHUNK, 2 * NB), BF16), pltpu.SemaphoreType.DMA((2,))],
        flops=20 * NB * M,
        nbytes=4 * NB * M,
        out_specs=[HBM],
    )(obs_xy, xy)
    recv = exchange(piece, "z")
    (piece,) = call("pair", pair_kernel, [((XC, NZ // 2, S, CAP), F32)], [VMEM])(recv)
    recv = exchange(piece, ("x", "core"))
    return call("final", final_kernel, [((S, NB), F32)], [VMEM] * 3, flops=4 * 2 * S * NB * M, nbytes=4 * NB * M)(
        recv, tile, field
    )[0]


def solution(mesh):
    grid = Mesh(mesh.devices.reshape(NZ, 4, 2, 4), ("z", "x", "core", "y"))
    leaf = ("z", "x", "core")
    in_specs = (
        P("y", leaf),
        P(leaf, None),
        P(None, None, leaf),
        P(None, leaf),
        P(leaf),
        P(leaf),
        P(leaf),
        P(("z", "x", "core", "y"), None),
    )

    return jax.shard_map(body, mesh=grid, in_specs=in_specs, out_specs=P("y", leaf), check_vma=False)
```

```python
import math

import jax
import jax.numpy as jnp
from jax import lax
from jax.experimental import pallas as pl
from jax.experimental.pallas import tpu as pltpu
from jax.sharding import Mesh, PartitionSpec as P


corr_length = 0.15
SCALE = math.log2(math.e) / corr_length
LEVELS = 7
R = 64
XC = 8
NZ = 16
S = 16
NB = 256
CAP = 128
M = 8192
ROWS = 64
F32 = jnp.float32
BF16 = jnp.bfloat16

VMEM = pl.BlockSpec(memory_space=pltpu.VMEM)
HBM = pl.BlockSpec(memory_space=pltpu.MemorySpace.HBM)
SMEM = pl.BlockSpec(memory_space=pltpu.SMEM)
NT = (((1,), (1,)), ((), ()))

VMEM_MIB = {'local': 2, 'observed': 1, 'near': 2, 'field': 4, 'inverse': 10, 'join': 4, 'spread': 4, 'coef': 10, 'cross': 8, 'own_half': 14, 'other_half': 10}


def dot(a, b, dims=(((1,), (0,)), ((), ()))):
    return lax.dot_general(a, b, dims, preferred_element_type=F32)


def split2(v):
    hi = v.astype(BF16)
    return hi, (v - hi.astype(F32)).astype(BF16)


def split3(v):
    hi = v.astype(BF16)
    rest = v - hi.astype(F32)
    mid = rest.astype(BF16)
    return hi, mid, (rest - mid.astype(F32)).astype(BF16)


def fetch(sems, pairs):
    copies = [pltpu.make_async_copy(src, dst, sems.at[i]) for i, (src, dst) in enumerate(pairs)]
    for copy in copies:
        copy.start()
    for copy in copies:
        copy.wait()


def project_kernel(z_ref, basis_ref, count_ref, out_ref):
    proj = dot(z_ref[...], basis_ref[...], NT)
    count = jnp.full((S, R), count_ref[0], jnp.int32).astype(F32)
    piece = jnp.concatenate([proj, count], axis=1)
    for q in range(XC):
        out_ref[q] = piece


def observed_kernel(value_hbm, value_ref, sems):
    fetch(sems, [(value_hbm, value_ref)])


def local_kernel(
    z_ref, diag_hbm, xy_hbm, site_hbm, basis_hbm, field_ref, pick_ref, xy_at_ref, xy_ref, basis_ref, diag_ref, site_ref, sems
):
    fetch(sems, [(diag_hbm, diag_ref), (xy_hbm, xy_ref), (site_hbm, site_ref), (basis_hbm, basis_ref)])
    field_ref[...] = dot(z_ref[...], diag_ref[...])
    site = lax.broadcasted_iota(jnp.int32, (NB, CAP), 0)
    pick = jnp.where(site == site_ref[...], 1.0, 0.0).astype(BF16)
    pick_ref[...] = pick
    known = jnp.concatenate([xy_ref[...] * SCALE, jnp.zeros((6, NB), F32)], axis=0)
    at = dot(jnp.concatenate(split3(known), axis=0), pick)
    at = (at[16:] + at[8:16]) + at[:8]
    half = [at[:2, :R], at[:2, R:]]
    xy_at_ref[...] = jnp.concatenate([half[0][0:1], half[1][0:1], half[0][1:2], half[1][1:2], jnp.zeros((12, R), F32)], axis=0)


def near_kernel(recv_ref, xy_at_ref, near_ref, out_ref):
    me = lax.axis_index("x") * 2 + lax.axis_index("core")
    my_z = lax.axis_index("z")
    level = lax.broadcasted_iota(jnp.int32, (S, 512), 1) // R
    row = lax.broadcasted_iota(jnp.int32, (S, R), 0)
    total = jnp.zeros((S, 512), F32)
    extra = xy_at_ref[...]
    for q in range(XC):
        apart = me ^ q
        own_level = jnp.where(apart == 1, 0, jnp.where(apart < 4, 1, 2))
        own_level = jnp.where(apart == 0, -1, own_level)
        got = recv_ref[q]
        total = total + jnp.where((level == own_level) | (level >= 3), got, 0.0)
        extra = jnp.where(row == q + 8, got[:, LEVELS * R :], extra)
    near_ref[...] = total
    parts = [jnp.concatenate([total[:, (3 + k) * R : (4 + k) * R], extra], axis=1) for k in range(4)]
    for z in range(NZ):
        apart = my_z ^ z
        out_ref[z] = jnp.where(apart >= 8, parts[3], jnp.where(apart >= 4, parts[2], jnp.where(apart >= 2, parts[1], parts[0])))


def field_kernel(recv_ref, near_ref, local_ref, basis_ref, pick_ref, value_ref, field_ref, out_ref):
    my_z = lax.axis_index("z")
    far = [jnp.zeros((S, CAP), F32) for _ in range(4)]
    for z in range(NZ):
        apart = my_z ^ z
        got = recv_ref[z]
        for k in range(4):
            mine = (apart >= 2**k) & (apart < 2 ** (k + 1))
            far[k] = far[k] + jnp.where(mine, got, 0.0)
    coef = jnp.concatenate([near_ref[:, : 3 * R]] + [f[:, :R] for f in far], axis=1)
    level = lax.broadcasted_iota(jnp.int32, (S, LEVELS * R), 1) // R
    factor = jnp.zeros((S, LEVELS * R), F32)
    for k in range(LEVELS):
        factor = jnp.where(level == k, 0.5 / math.sqrt(R * NB * 2.0**k), factor)
    coef = coef * factor
    low = dot(jnp.concatenate(split3(coef), axis=0), basis_ref[...])
    field = local_ref[...] + ((low[2 * S :] + low[S : 2 * S]) + low[:S])
    field_ref[...] = field
    at = dot(jnp.concatenate(split3(field), axis=0), pick_ref[...])
    residual = value_ref[...] - ((at[2 * S :] + at[S : 2 * S]) + at[:S])
    for z in range(NZ):
        out_ref[z] = residual


def spread_kernel(recv_ref, extra_ref, out_ref):
    for x in range(4):
        for z in range(NZ):
            out_ref[x, S * z : S * (z + 1)] = recv_ref[z]
    for z in range(0, NZ, 4):
        rows = []
        for zz in range(z, z + 4):
            rows += [jnp.concatenate([extra_ref[zz, 2 * i : 2 * i + 1, R:], extra_ref[zz, 2 * i + 1 : 2 * i + 2, R:]], axis=1) for i in range(2)]
        rows = jnp.concatenate(rows, axis=0)
        for x in range(4):
            out_ref[x, S * NZ + 2 * z : S * NZ + 2 * z + 8] = rows


def join_kernel(own_hbm, next_hbm, out_hbm, held, sems):
    fetch(sems, [(own_hbm, held.at[0]), (next_hbm, held.at[1])])
    fetch(sems, [(held.at[d], out_hbm.at[d]) for d in range(2)])


def inverse_kernel(near_hbm, far_hbm, out_ref, held, sems):
    fetch(sems, [(ref.at[d], held.at[2 * i + d]) for i, ref in enumerate((near_hbm, far_hbm)) for d in range(2)])
    my_y = lax.axis_index("y")

    def one_part(j, carry):
        at = pl.multiple_of(j * 256, 256)
        got = [held[d, :, pl.ds(at, 256)] for d in range(4)]
        rows = []
        for y in range(4):
            apart = my_y ^ y
            rows.append(jnp.where(apart >= 2, jnp.where(apart == 2, got[2], got[3]), jnp.where(apart == 0, got[0], got[1])))
        rows = jnp.concatenate(rows, axis=0)
        hi = rows.astype(BF16).astype(F32)
        out_ref[pl.ds(at, 256)] = jnp.transpose(jnp.concatenate([hi, rows - hi], axis=0)).astype(BF16)
        return carry

    lax.fori_loop(0, M // 256, one_part, 0, unroll=4)


def coef_kernel(base_ref, count_ref, own_ref, other_ref, inv_ref, out_ref, xy_ref, packed):
    core = lax.axis_index("core")
    lane = lax.broadcasted_iota(jnp.int32, (S, CAP), 1)

    def one_column(x, carry):
        for ref, c in ((own_ref, core), (other_ref, 1 - core)):
            for z in range(NZ):
                p = 8 * z + 2 * x + c
                base, count = base_ref[p], count_ref[p]
                shift = base % CAP
                start = pl.multiple_of(base - shift, CAP)
                end = shift + count
                first = (lane >= shift) & (lane < end)
                second = lane < end - CAP
                got = pltpu.roll(ref[x, S * z : S * (z + 1)], shift, 1)
                pltpu.store(packed.at[:, pl.ds(start, CAP)], got, mask=first)
                pltpu.store(packed.at[:, pl.ds(start + CAP, CAP)], got, mask=second)
                got = pltpu.roll(ref[x, S * NZ + 2 * z : S * NZ + 2 * z + 2], shift, 1)
                pltpu.store(xy_ref.at[:, pl.ds(start, CAP)], got, mask=first[:2])
                pltpu.store(xy_ref.at[:, pl.ds(start + CAP, CAP)], got, mask=second[:2])
        return carry

    lax.fori_loop(0, 4, one_column, 0)
    acc = jnp.zeros((2 * S, 2 * ROWS), F32)
    width = 1024
    for k in range(0, M, width):
        acc = acc + dot(jnp.concatenate(split2(packed[:, k : k + width]), axis=0), inv_ref[k : k + width])
    coef = acc[:S] + acc[S:]
    coef = coef[:, :ROWS] + coef[:, ROWS:]
    piece = jnp.concatenate([coef[: S // 2], coef[S // 2 :]], axis=1)
    for i in range(M // CAP):
        out_ref[i] = piece


HALF = M // 2
CHUNK = 256
KEPT = 10


def cross_kernel(obs_ref, xy_ref, kept_ref, own_hbm, other_hbm, buf, sems):
    core = lax.axis_index("core")
    sx = xy_ref[0:1] * SCALE
    sy = xy_ref[1:2] * SCALE

    def rows(i):
        return pl.ds(pl.multiple_of(i * CHUNK, CHUNK), CHUNK)

    def copies(i, slot, own_ref, first):
        return [
            pltpu.make_async_copy(buf.at[slot, 0], own_ref.at[rows(i - first)], sems.at[slot, 0]),
            pltpu.make_async_copy(buf.at[slot, 1], other_hbm.at[rows(i)], sems.at[slot, 1]),
        ]

    def step(own_ref, first):
        def run(i, carry):
            slot = i % 2

            @pl.when(i > 1)
            def _():
                for copy in copies(first, slot, own_ref, first):
                    copy.wait()

            for m in range(4):
                at = pl.multiple_of(2 * CHUNK * i + CAP * m, CAP)
                ox = jnp.transpose(jnp.broadcast_to(obs_ref[0:1, pl.ds(at, CAP)], (CAP, CAP)))
                oy = jnp.transpose(jnp.broadcast_to(obs_ref[1:2, pl.ds(at, CAP)], (CAP, CAP)))
                for h in range(0, NB, CAP):
                    dx = ox - sx[:, h : h + CAP]
                    dy = oy - sy[:, h : h + CAP]
                    square = jnp.maximum(dx * dx + dy * dy, 1e-30)
                    hi, lo = split2(jnp.exp2(-(square * lax.rsqrt(square))))
                    for c in range(2):
                        for part, left in ((hi, h), (lo, NB + h)):
                            buf[slot, core ^ c, ROWS * m : ROWS * (m + 1), left : left + CAP] = part[ROWS * c : ROWS * (c + 1)]
            for copy in copies(i, slot, own_ref, first):
                copy.start()
            return carry

        return run

    steps = HALF // CHUNK
    lax.fori_loop(0, KEPT, step(kept_ref, 0), 0)
    lax.fori_loop(KEPT, steps, step(own_hbm, KEPT), 0)
    for i in range(steps - 2, steps):
        for copy in copies(i, i % 2, own_hbm, KEPT):
            copy.wait()


def coef_chunk(pieces_ref, k):
    lane = lax.broadcasted_iota(jnp.int32, (S // 2, CAP), 1)
    blocks = []
    for m in range(4 * k, 4 * k + 4, 2):
        even, odd = pieces_ref[m], pieces_ref[m + 1]
        first = jnp.where(lane < ROWS, even, pltpu.roll(odd, ROWS, 1))
        second = jnp.where(lane < ROWS, pltpu.roll(even, ROWS, 1), odd)
        blocks.append(jnp.concatenate([first, second], axis=0))
    return jnp.concatenate(split2(jnp.concatenate(blocks, axis=1)), axis=0)


def fold(acc):
    acc = acc[:S] + acc[S:]
    return acc[:, :NB] + acc[:, NB:]


def own_half_kernel(pieces_ref, kept_ref, own_hbm, other_hbm, out_ref, other_ref, buf, sems, other_sem):
    steps = HALF // CHUNK
    rows = [pl.ds(i * CHUNK, CHUNK) for i in range(steps)]
    copies = [pltpu.make_async_copy(own_hbm.at[rows[i]], buf.at[i], sems.at[i]) for i in range(steps - KEPT)]
    others = [pltpu.make_async_copy(other_hbm.at[rows[i]], other_ref.at[rows[i]], other_sem.at[i]) for i in range(steps)]
    for copy in copies + others:
        copy.start()
    acc = jnp.zeros((2 * S, 2 * NB), F32)
    for k in range(steps):
        left = coef_chunk(pieces_ref, k)
        if k < KEPT:
            right = kept_ref[rows[k]]
        else:
            copies[k - KEPT].wait()
            right = buf[k - KEPT]
        acc = acc + dot(left, right)
    out_ref[...] = fold(acc)
    for copy in others:
        copy.wait()


def other_half_kernel(pieces_ref, tile_ref, partial_ref, field_ref, out_ref):
    acc = jnp.zeros((2 * S, 2 * NB), F32)
    for k in range(HALF // CHUNK):
        acc = acc + dot(coef_chunk(pieces_ref, k), tile_ref[k * CHUNK : (k + 1) * CHUNK])
    out_ref[...] = field_ref[...] + (partial_ref[...] + fold(acc))


def call(name, kernel, out, specs, scratch=(), flops=0, nbytes=0, out_specs=None):
    out_specs = out_specs or [VMEM] * len(out)
    shapes = [pltpu.MemorySpace.HBM(s, d) if spec is HBM else jax.ShapeDtypeStruct(s, d) for (s, d), spec in zip(out, out_specs)]
    made = pl.pallas_call(
        kernel,
        out_shape=shapes,
        in_specs=specs,
        out_specs=out_specs,
        scratch_shapes=list(scratch),
        compiler_params=pltpu.CompilerParams(vmem_limit_bytes=VMEM_MIB[name] << 20 if name in VMEM_MIB else None),
        cost_estimate=pl.CostEstimate(flops=flops, bytes_accessed=nbytes, transcendentals=0),
    )

    def run(*args):
        return made(*(pltpu.with_memory_space_constraint(a, pltpu.MemorySpace.HBM) if spec is HBM else a for a, spec in zip(args, specs)))

    return run


def exchange(piece, axes):
    return lax.all_to_all(piece, axes, 0, 0, tiled=True)


def body(samples_z, diag_block, level_basis, site_xy, obs_site, obs_value, obs_count, inverse_rows):
    basis = level_basis.reshape(LEVELS * R, NB)
    block = lax.ppermute(inverse_rows, "y", [(y, y ^ 1) for y in range(4)])
    (pair,) = call(
        "join",
        join_kernel,
        [((2, S, M), F32)],
        [HBM, HBM],
        [pltpu.VMEM((2, S, M), F32), pltpu.SemaphoreType.DMA((2,))],
        out_specs=[HBM],
    )(inverse_rows, block)
    far_pair = lax.ppermute(pair, "y", [(y, y ^ 2) for y in range(4)])

    (piece,) = call("project", project_kernel, [((XC, S, 512), F32)], [VMEM, VMEM, SMEM])(samples_z, basis, obs_count)
    recv = exchange(piece, ("x", "core"))
    local, pick, xy_at, xy, basis = call(
        "local",
        local_kernel,
        [((S, NB), F32), ((NB, CAP), BF16), ((S, R), F32), ((2, NB), F32), ((LEVELS * R, NB), BF16)],
        [VMEM] + [HBM] * 4,
        [pltpu.VMEM((NB, NB), BF16), pltpu.VMEM((1, CAP), jnp.int32), pltpu.SemaphoreType.DMA((4,))],
        flops=2 * S * NB * NB,
        nbytes=1 << 18,
    )(samples_z, diag_block, site_xy, obs_site.reshape(1, CAP), basis)
    (value,) = call("observed", observed_kernel, [((1, CAP), F32)], [HBM], [pltpu.SemaphoreType.DMA((1,))])(obs_value.reshape(1, CAP))
    near, piece = call("near", near_kernel, [((S, 512), F32), ((NZ, S, CAP), F32)], [VMEM] * 2)(recv, xy_at)
    extra = exchange(piece, "z")
    counts = extra[:, 8:, R].reshape(XC * NZ)
    order = jnp.arange(XC * NZ, dtype=jnp.int32)
    base = jnp.sum(jnp.where(order[None, :] < order[:, None], counts[None, :], 0.0), axis=1).astype(jnp.int32)
    counts = counts.astype(jnp.int32)
    field, piece = call("field", field_kernel, [((S, NB), F32), ((NZ, S, CAP), F32)], [VMEM] * 6)(
        extra, near, local, basis, pick, value
    )
    (inv,) = call(
        "inverse",
        inverse_kernel,
        [((M, 2 * ROWS), BF16)],
        [HBM] * 2,
        [pltpu.VMEM((4, S, M), F32), pltpu.SemaphoreType.DMA((4,))],
        flops=20 * ROWS * M,
        nbytes=8 * ROWS * M,
    )(pair, far_pair)
    recv = exchange(piece, "z")
    (piece,) = call("spread", spread_kernel, [((4, 18 * NZ, CAP), F32)], [VMEM] * 2)(recv, extra)
    own = exchange(piece, "x")
    other = lax.ppermute(own, "core", [(0, 1), (1, 0)])
    piece, obs_xy = call(
        "coef",
        coef_kernel,
        [((M // CAP, S // 2, CAP), F32), ((2, M + 2 * CAP), F32)],
        [SMEM, SMEM, VMEM, VMEM, VMEM],
        [pltpu.VMEM((S, M + 2 * CAP), F32)],
        flops=4 * 2 * S * ROWS * M,
        nbytes=4 * ROWS * M,
    )(base, counts, own, other, inv)
    kept, own_tile, other_tile = call(
        "cross",
        cross_kernel,
        [((KEPT * CHUNK, 2 * NB), BF16), ((HALF - KEPT * CHUNK, 2 * NB), BF16), ((HALF, 2 * NB), BF16)],
        [VMEM, VMEM],
        [pltpu.VMEM((2, 2, CHUNK, 2 * NB), BF16), pltpu.SemaphoreType.DMA((2, 2))],
        flops=20 * NB * M,
        nbytes=4 * NB * M,
        out_specs=[VMEM, HBM, HBM],
    )(obs_xy, xy)
    own = exchange(piece, ("z", "x"))
    other = lax.ppermute(own, "core", [(0, 1), (1, 0)])
    streamed = HALF // CHUNK - KEPT
    partial, other_tile = call(
        "own_half",
        own_half_kernel,
        [((S, NB), F32), ((HALF, 2 * NB), BF16)],
        [VMEM, VMEM, HBM, HBM],
        [
            pltpu.VMEM((streamed, CHUNK, 2 * NB), BF16),
            pltpu.SemaphoreType.DMA((streamed,)),
            pltpu.SemaphoreType.DMA((HALF // CHUNK,)),
        ],
        flops=2 * 2 * S * NB * M,
        nbytes=4 * NB * M,
    )(own, kept, own_tile, other_tile)
    return call("other_half", other_half_kernel, [((S, NB), F32)], [VMEM] * 4, flops=2 * 2 * S * NB * M, nbytes=2 * NB * M)(
        other, other_tile, partial, field
    )[0]


def solution(mesh):
    grid = Mesh(mesh.devices.reshape(NZ, 4, 2, 4), ("z", "x", "core", "y"))
    leaf = ("z", "x", "core")
    in_specs = (
        P("y", leaf),
        P(leaf, None),
        P(None, None, leaf),
        P(None, leaf),
        P(leaf),
        P(leaf),
        P(leaf),
        P(("z", "x", "core", "y"), None),
    )

    return jax.shard_map(body, mesh=grid, in_specs=in_specs, out_specs=P("y", leaf), check_vma=False)
```

```python
import math

import jax
import jax.numpy as jnp
from jax import lax
from jax.experimental import pallas as pl
from jax.experimental.pallas import tpu as pltpu
from jax.sharding import Mesh, PartitionSpec as P


corr_length = 0.15
SCALE = math.log2(math.e) / corr_length
LEVELS = 7
R = 64
XC = 8
NZ = 16
S = 16
NB = 256
CAP = 128
M = 8192
ROWS = 64
F32 = jnp.float32
BF16 = jnp.bfloat16

VMEM = pl.BlockSpec(memory_space=pltpu.VMEM)
HBM = pl.BlockSpec(memory_space=pltpu.MemorySpace.HBM)
SMEM = pl.BlockSpec(memory_space=pltpu.SMEM)
NT = (((1,), (1,)), ((), ()))

VMEM_MIB = {'local': 2, 'near': 2, 'field': 4, 'inverse': 10, 'join': 4, 'spread': 4, 'coef': 10, 'cross': 8, 'own_half': 14, 'other_half': 10}


def dot(a, b, dims=(((1,), (0,)), ((), ()))):
    return lax.dot_general(a, b, dims, preferred_element_type=F32)


def split2(v):
    hi = v.astype(BF16)
    return hi, (v - hi.astype(F32)).astype(BF16)


def split3(v):
    hi = v.astype(BF16)
    rest = v - hi.astype(F32)
    mid = rest.astype(BF16)
    return hi, mid, (rest - mid.astype(F32)).astype(BF16)


def fetch(sems, pairs):
    copies = [pltpu.make_async_copy(src, dst, sems.at[i]) for i, (src, dst) in enumerate(pairs)]
    for copy in copies:
        copy.start()
    for copy in copies:
        copy.wait()


def project_kernel(z_ref, basis_ref, count_ref, out_ref):
    proj = dot(z_ref[...], basis_ref[...], NT)
    count = jnp.full((S, R), count_ref[0], jnp.int32).astype(F32)
    piece = jnp.concatenate([proj, count], axis=1)
    for q in range(XC):
        out_ref[q] = piece


def local_kernel(
    z_ref, diag_hbm, xy_hbm, site_hbm, basis_hbm, value_hbm, field_ref, pick_ref, xy_at_ref, xy_ref, basis_ref, value_ref, diag_ref, site_ref, sems
):
    fetch(sems, [(diag_hbm, diag_ref), (xy_hbm, xy_ref), (site_hbm, site_ref), (basis_hbm, basis_ref), (value_hbm, value_ref)])
    field_ref[...] = dot(z_ref[...], diag_ref[...])
    site = lax.broadcasted_iota(jnp.int32, (NB, CAP), 0)
    pick = jnp.where(site == site_ref[...], 1.0, 0.0).astype(BF16)
    pick_ref[...] = pick
    known = jnp.concatenate([xy_ref[...] * SCALE, jnp.zeros((6, NB), F32)], axis=0)
    at = dot(jnp.concatenate(split3(known), axis=0), pick)
    at = (at[16:] + at[8:16]) + at[:8]
    half = [at[:2, :R], at[:2, R:]]
    xy_at_ref[...] = jnp.concatenate([half[0][0:1], half[1][0:1], half[0][1:2], half[1][1:2], jnp.zeros((12, R), F32)], axis=0)


def near_kernel(recv_ref, xy_at_ref, near_ref, out_ref):
    me = lax.axis_index("x") * 2 + lax.axis_index("core")
    my_z = lax.axis_index("z")
    level = lax.broadcasted_iota(jnp.int32, (S, 512), 1) // R
    row = lax.broadcasted_iota(jnp.int32, (S, R), 0)
    total = jnp.zeros((S, 512), F32)
    extra = xy_at_ref[...]
    for q in range(XC):
        apart = me ^ q
        own_level = jnp.where(apart == 1, 0, jnp.where(apart < 4, 1, 2))
        own_level = jnp.where(apart == 0, -1, own_level)
        got = recv_ref[q]
        total = total + jnp.where((level == own_level) | (level >= 3), got, 0.0)
        extra = jnp.where(row == q + 8, got[:, LEVELS * R :], extra)
    near_ref[...] = total
    parts = [jnp.concatenate([total[:, (3 + k) * R : (4 + k) * R], extra], axis=1) for k in range(4)]
    for z in range(NZ):
        apart = my_z ^ z
        out_ref[z] = jnp.where(apart >= 8, parts[3], jnp.where(apart >= 4, parts[2], jnp.where(apart >= 2, parts[1], parts[0])))


def field_kernel(recv_ref, near_ref, local_ref, basis_ref, pick_ref, value_ref, field_ref, out_ref):
    my_z = lax.axis_index("z")
    far = [jnp.zeros((S, CAP), F32) for _ in range(4)]
    for z in range(NZ):
        apart = my_z ^ z
        got = recv_ref[z]
        for k in range(4):
            mine = (apart >= 2**k) & (apart < 2 ** (k + 1))
            far[k] = far[k] + jnp.where(mine, got, 0.0)
    coef = jnp.concatenate([near_ref[:, : 3 * R]] + [f[:, :R] for f in far], axis=1)
    level = lax.broadcasted_iota(jnp.int32, (S, LEVELS * R), 1) // R
    factor = jnp.zeros((S, LEVELS * R), F32)
    for k in range(LEVELS):
        factor = jnp.where(level == k, 0.5 / math.sqrt(R * NB * 2.0**k), factor)
    coef = coef * factor
    low = dot(jnp.concatenate(split3(coef), axis=0), basis_ref[...])
    field = local_ref[...] + ((low[2 * S :] + low[S : 2 * S]) + low[:S])
    field_ref[...] = field
    at = dot(jnp.concatenate(split3(field), axis=0), pick_ref[...])
    residual = value_ref[...] - ((at[2 * S :] + at[S : 2 * S]) + at[:S])
    for z in range(NZ):
        out_ref[z] = residual


def spread_kernel(recv_ref, extra_ref, out_ref):
    for x in range(4):
        for z in range(NZ):
            out_ref[x, S * z : S * (z + 1)] = recv_ref[z]
    for z in range(0, NZ, 4):
        rows = []
        for zz in range(z, z + 4):
            rows += [jnp.concatenate([extra_ref[zz, 2 * i : 2 * i + 1, R:], extra_ref[zz, 2 * i + 1 : 2 * i + 2, R:]], axis=1) for i in range(2)]
        rows = jnp.concatenate(rows, axis=0)
        for x in range(4):
            out_ref[x, S * NZ + 2 * z : S * NZ + 2 * z + 8] = rows


def join_kernel(own_hbm, next_ref, out_hbm, held, sems):
    arrived = pltpu.make_async_copy(next_ref, out_hbm.at[1], sems.at[1])
    arrived.start()
    fetch(sems, [(own_hbm, held)])
    fetch(sems, [(held, out_hbm.at[0])])
    arrived.wait()


def inverse_kernel(near_hbm, far_hbm, out_ref, held, sems):
    fetch(sems, [(ref.at[d], held.at[2 * i + d]) for i, ref in enumerate((near_hbm, far_hbm)) for d in range(2)])
    my_y = lax.axis_index("y")

    def one_part(j, carry):
        at = pl.multiple_of(j * 256, 256)
        got = [held[d, :, pl.ds(at, 256)] for d in range(4)]
        rows = []
        for y in range(4):
            apart = my_y ^ y
            rows.append(jnp.where(apart >= 2, jnp.where(apart == 2, got[2], got[3]), jnp.where(apart == 0, got[0], got[1])))
        rows = jnp.concatenate(rows, axis=0)
        hi = rows.astype(BF16).astype(F32)
        out_ref[pl.ds(at, 256)] = jnp.transpose(jnp.concatenate([hi, rows - hi], axis=0)).astype(BF16)
        return carry

    lax.fori_loop(0, M // 256, one_part, 0, unroll=4)


def coef_kernel(base_ref, count_ref, own_ref, other_ref, inv_ref, out_ref, xy_ref, packed):
    core = lax.axis_index("core")
    lane = lax.broadcasted_iota(jnp.int32, (S, CAP), 1)

    def one_column(x, carry):
        for ref, c in ((own_ref, core), (other_ref, 1 - core)):
            for z in range(NZ):
                p = 8 * z + 2 * x + c
                base, count = base_ref[p], count_ref[p]
                shift = base % CAP
                start = pl.multiple_of(base - shift, CAP)
                end = shift + count
                first = (lane >= shift) & (lane < end)
                second = lane < end - CAP
                got = pltpu.roll(ref[x, S * z : S * (z + 1)], shift, 1)
                pltpu.store(packed.at[:, pl.ds(start, CAP)], got, mask=first)
                pltpu.store(packed.at[:, pl.ds(start + CAP, CAP)], got, mask=second)
                got = pltpu.roll(ref[x, S * NZ + 2 * z : S * NZ + 2 * z + 2], shift, 1)
                pltpu.store(xy_ref.at[:, pl.ds(start, CAP)], got, mask=first[:2])
                pltpu.store(xy_ref.at[:, pl.ds(start + CAP, CAP)], got, mask=second[:2])
        return carry

    lax.fori_loop(0, 4, one_column, 0)
    acc = jnp.zeros((2 * S, 2 * ROWS), F32)
    width = 1024
    for k in range(0, M, width):
        acc = acc + dot(jnp.concatenate(split2(packed[:, k : k + width]), axis=0), inv_ref[k : k + width])
    coef = acc[:S] + acc[S:]
    coef = coef[:, :ROWS] + coef[:, ROWS:]
    piece = jnp.concatenate([coef[: S // 2], coef[S // 2 :]], axis=1)
    for i in range(M // CAP):
        out_ref[i] = piece


HALF = M // 2
CHUNK = 256
KEPT = 12


def cross_kernel(obs_ref, xy_ref, kept_ref, own_hbm, other_hbm, buf, sems):
    core = lax.axis_index("core")
    sx = xy_ref[0:1] * SCALE
    sy = xy_ref[1:2] * SCALE

    def rows(i):
        return pl.ds(pl.multiple_of(i * CHUNK, CHUNK), CHUNK)

    def copies(i, slot, own_ref, first):
        return [
            pltpu.make_async_copy(buf.at[slot, 0], own_ref.at[rows(i - first)], sems.at[slot, 0]),
            pltpu.make_async_copy(buf.at[slot, 1], other_hbm.at[rows(i)], sems.at[slot, 1]),
        ]

    def step(own_ref, first):
        def run(i, carry):
            slot = i % 2

            @pl.when(i > 1)
            def _():
                for copy in copies(first, slot, own_ref, first):
                    copy.wait()

            for m in range(4):
                at = pl.multiple_of(2 * CHUNK * i + CAP * m, CAP)
                ox = jnp.transpose(jnp.broadcast_to(obs_ref[0:1, pl.ds(at, CAP)], (CAP, CAP)))
                oy = jnp.transpose(jnp.broadcast_to(obs_ref[1:2, pl.ds(at, CAP)], (CAP, CAP)))
                for h in range(0, NB, CAP):
                    dx = ox - sx[:, h : h + CAP]
                    dy = oy - sy[:, h : h + CAP]
                    square = jnp.maximum(dx * dx + dy * dy, 1e-30)
                    hi, lo = split2(jnp.exp2(-(square * lax.rsqrt(square))))
                    for c in range(2):
                        for part, left in ((hi, h), (lo, NB + h)):
                            buf[slot, core ^ c, ROWS * m : ROWS * (m + 1), left : left + CAP] = part[ROWS * c : ROWS * (c + 1)]
            for copy in copies(i, slot, own_ref, first):
                copy.start()
            return carry

        return run

    steps = HALF // CHUNK
    lax.fori_loop(0, KEPT, step(kept_ref, 0), 0)
    lax.fori_loop(KEPT, steps, step(own_hbm, KEPT), 0)
    for i in range(steps - 2, steps):
        for copy in copies(i, i % 2, own_hbm, KEPT):
            copy.wait()


def coef_chunk(pieces_ref, k):
    lane = lax.broadcasted_iota(jnp.int32, (S // 2, CAP), 1)
    blocks = []
    for m in range(4 * k, 4 * k + 4, 2):
        even, odd = pieces_ref[m], pieces_ref[m + 1]
        first = jnp.where(lane < ROWS, even, pltpu.roll(odd, ROWS, 1))
        second = jnp.where(lane < ROWS, pltpu.roll(even, ROWS, 1), odd)
        blocks.append(jnp.concatenate([first, second], axis=0))
    return jnp.concatenate(split2(jnp.concatenate(blocks, axis=1)), axis=0)


def fold(acc):
    acc = acc[:S] + acc[S:]
    return acc[:, :NB] + acc[:, NB:]


def own_half_kernel(pieces_ref, kept_ref, own_hbm, other_hbm, out_ref, other_ref, buf, sems, other_sem):
    steps = HALF // CHUNK
    rows = [pl.ds(i * CHUNK, CHUNK) for i in range(steps)]
    copies = [pltpu.make_async_copy(own_hbm.at[rows[i]], buf.at[i], sems.at[i]) for i in range(steps - KEPT)]
    others = [pltpu.make_async_copy(other_hbm.at[rows[i]], other_ref.at[rows[i]], other_sem.at[i]) for i in range(steps)]
    for copy in copies + others:
        copy.start()
    acc = jnp.zeros((2 * S, 2 * NB), F32)
    for k in range(steps):
        left = coef_chunk(pieces_ref, k)
        if k < KEPT:
            right = kept_ref[rows[k]]
        else:
            copies[k - KEPT].wait()
            right = buf[k - KEPT]
        acc = acc + dot(left, right)
    out_ref[...] = fold(acc)
    for copy in others:
        copy.wait()


def other_half_kernel(pieces_ref, tile_ref, partial_ref, field_ref, out_ref):
    acc = jnp.zeros((2 * S, 2 * NB), F32)
    for k in range(HALF // CHUNK):
        acc = acc + dot(coef_chunk(pieces_ref, k), tile_ref[k * CHUNK : (k + 1) * CHUNK])
    out_ref[...] = field_ref[...] + (partial_ref[...] + fold(acc))


def call(name, kernel, out, specs, scratch=(), flops=0, nbytes=0, out_specs=None):
    out_specs = out_specs or [VMEM] * len(out)
    shapes = [pltpu.MemorySpace.HBM(s, d) if spec is HBM else jax.ShapeDtypeStruct(s, d) for (s, d), spec in zip(out, out_specs)]
    made = pl.pallas_call(
        kernel,
        out_shape=shapes,
        in_specs=specs,
        out_specs=out_specs,
        scratch_shapes=list(scratch),
        compiler_params=pltpu.CompilerParams(vmem_limit_bytes=VMEM_MIB[name] << 20 if name in VMEM_MIB else None),
        cost_estimate=pl.CostEstimate(flops=flops, bytes_accessed=nbytes, transcendentals=0),
    )

    def run(*args):
        return made(*(pltpu.with_memory_space_constraint(a, pltpu.MemorySpace.HBM) if spec is HBM else a for a, spec in zip(args, specs)))

    return run


def exchange(piece, axes):
    return lax.all_to_all(piece, axes, 0, 0, tiled=True)


def body(samples_z, diag_block, level_basis, site_xy, obs_site, obs_value, obs_count, inverse_rows):
    basis = level_basis.reshape(LEVELS * R, NB)
    block = lax.ppermute(inverse_rows, "y", [(y, y ^ 1) for y in range(4)])
    (pair,) = call(
        "join",
        join_kernel,
        [((2, S, M), F32)],
        [HBM, VMEM],
        [pltpu.VMEM((S, M), F32), pltpu.SemaphoreType.DMA((2,))],
        out_specs=[HBM],
    )(inverse_rows, block)
    far_pair = lax.ppermute(pair, "y", [(y, y ^ 2) for y in range(4)])

    (piece,) = call("project", project_kernel, [((XC, S, 512), F32)], [VMEM, VMEM, SMEM])(samples_z, basis, obs_count)
    recv = exchange(piece, ("x", "core"))
    local, pick, xy_at, xy, basis, value = call(
        "local",
        local_kernel,
        [((S, NB), F32), ((NB, CAP), BF16), ((S, R), F32), ((2, NB), F32), ((LEVELS * R, NB), BF16), ((1, CAP), F32)],
        [VMEM] + [HBM] * 5,
        [pltpu.VMEM((NB, NB), BF16), pltpu.VMEM((1, CAP), jnp.int32), pltpu.SemaphoreType.DMA((5,))],
        flops=2 * S * NB * NB,
        nbytes=1 << 18,
    )(samples_z, diag_block, site_xy, obs_site.reshape(1, CAP), basis, obs_value.reshape(1, CAP))
    near, piece = call("near", near_kernel, [((S, 512), F32), ((NZ, S, CAP), F32)], [VMEM] * 2)(recv, xy_at)
    extra = exchange(piece, "z")
    counts = extra[:, 8:, R].reshape(XC * NZ)
    order = jnp.arange(XC * NZ, dtype=jnp.int32)
    base = jnp.sum(jnp.where(order[None, :] < order[:, None], counts[None, :], 0.0), axis=1).astype(jnp.int32)
    counts = counts.astype(jnp.int32)
    field, piece = call("field", field_kernel, [((S, NB), F32), ((NZ, S, CAP), F32)], [VMEM] * 6)(
        extra, near, local, basis, pick, value
    )
    (inv,) = call(
        "inverse",
        inverse_kernel,
        [((M, 2 * ROWS), BF16)],
        [HBM] * 2,
        [pltpu.VMEM((4, S, M), F32), pltpu.SemaphoreType.DMA((4,))],
        flops=20 * ROWS * M,
        nbytes=8 * ROWS * M,
    )(pair, far_pair)
    recv = exchange(piece, "z")
    (piece,) = call("spread", spread_kernel, [((4, 18 * NZ, CAP), F32)], [VMEM] * 2)(recv, extra)
    own = exchange(piece, "x")
    other = lax.ppermute(own, "core", [(0, 1), (1, 0)])
    piece, obs_xy = call(
        "coef",
        coef_kernel,
        [((M // CAP, S // 2, CAP), F32), ((2, M + 2 * CAP), F32)],
        [SMEM, SMEM, VMEM, VMEM, VMEM],
        [pltpu.VMEM((S, M + 2 * CAP), F32)],
        flops=4 * 2 * S * ROWS * M,
        nbytes=4 * ROWS * M,
    )(base, counts, own, other, inv)
    kept, own_tile, other_tile = call(
        "cross",
        cross_kernel,
        [((KEPT * CHUNK, 2 * NB), BF16), ((HALF - KEPT * CHUNK, 2 * NB), BF16), ((HALF, 2 * NB), BF16)],
        [VMEM, VMEM],
        [pltpu.VMEM((2, 2, CHUNK, 2 * NB), BF16), pltpu.SemaphoreType.DMA((2, 2))],
        flops=20 * NB * M,
        nbytes=4 * NB * M,
        out_specs=[VMEM, HBM, HBM],
    )(obs_xy, xy)
    own = exchange(piece, ("z", "x"))
    other = lax.ppermute(own, "core", [(0, 1), (1, 0)])
    streamed = HALF // CHUNK - KEPT
    partial, other_tile = call(
        "own_half",
        own_half_kernel,
        [((S, NB), F32), ((HALF, 2 * NB), BF16)],
        [VMEM, VMEM, HBM, HBM],
        [
            pltpu.VMEM((streamed, CHUNK, 2 * NB), BF16),
            pltpu.SemaphoreType.DMA((streamed,)),
            pltpu.SemaphoreType.DMA((HALF // CHUNK,)),
        ],
        flops=2 * 2 * S * NB * M,
        nbytes=4 * NB * M,
    )(own, kept, own_tile, other_tile)
    return call("other_half", other_half_kernel, [((S, NB), F32)], [VMEM] * 4, flops=2 * 2 * S * NB * M, nbytes=2 * NB * M)(
        other, other_tile, partial, field
    )[0]


def solution(mesh):
    grid = Mesh(mesh.devices.reshape(NZ, 4, 2, 4), ("z", "x", "core", "y"))
    leaf = ("z", "x", "core")
    in_specs = (
        P("y", leaf),
        P(leaf, None),
        P(None, None, leaf),
        P(None, leaf),
        P(leaf),
        P(leaf),
        P(leaf),
        P(("z", "x", "core", "y"), None),
    )

    return jax.shard_map(body, mesh=grid, in_specs=in_specs, out_specs=P("y", leaf), check_vma=False)
```

```python
import math

import jax
import jax.numpy as jnp
from jax import lax
from jax.experimental import pallas as pl
from jax.experimental.pallas import tpu as pltpu
from jax.sharding import Mesh, PartitionSpec as P


corr_length = 0.15
SCALE = math.log2(math.e) / corr_length
LEVELS = 7
R = 64
XC = 8
NZ = 16
S = 16
NB = 256
CAP = 128
M = 8192
ROWS = 64
F32 = jnp.float32
BF16 = jnp.bfloat16

VMEM = pl.BlockSpec(memory_space=pltpu.VMEM)
HBM = pl.BlockSpec(memory_space=pltpu.MemorySpace.HBM)
SMEM = pl.BlockSpec(memory_space=pltpu.SMEM)
NT = (((1,), (1,)), ((), ()))

VMEM_MIB = {'local': 2, 'near': 2, 'field': 4, 'inverse': 10, 'join': 4, 'spread': 4, 'pack': 4, 'coef': 10, 'cross': 8, 'own_half': 14, 'other_half': 10}


def dot(a, b, dims=(((1,), (0,)), ((), ()))):
    return lax.dot_general(a, b, dims, preferred_element_type=F32)


def split2(v):
    hi = v.astype(BF16)
    return hi, (v - hi.astype(F32)).astype(BF16)


def split3(v):
    hi = v.astype(BF16)
    rest = v - hi.astype(F32)
    mid = rest.astype(BF16)
    return hi, mid, (rest - mid.astype(F32)).astype(BF16)


def fetch(sems, pairs):
    copies = [pltpu.make_async_copy(src, dst, sems.at[i]) for i, (src, dst) in enumerate(pairs)]
    for copy in copies:
        copy.start()
    for copy in copies:
        copy.wait()


def project_kernel(z_ref, basis_ref, count_ref, out_ref):
    proj = dot(z_ref[...], basis_ref[...], NT)
    count = jnp.full((S, R), count_ref[0], jnp.int32).astype(F32)
    piece = jnp.concatenate([proj, count], axis=1)
    for q in range(XC):
        out_ref[q] = piece


def local_kernel(
    z_hbm, diag_hbm, xy_hbm, site_hbm, basis_hbm, value_hbm, field_ref, pick_ref, xy_at_ref, xy_ref, basis_ref, value_ref, diag_ref, site_ref, z_ref, sems
):
    fetch(sems, [(diag_hbm, diag_ref), (xy_hbm, xy_ref), (site_hbm, site_ref), (basis_hbm, basis_ref), (value_hbm, value_ref), (z_hbm, z_ref)])
    field_ref[...] = dot(z_ref[...], diag_ref[...])
    site = lax.broadcasted_iota(jnp.int32, (NB, CAP), 0)
    pick = jnp.where(site == site_ref[...], 1.0, 0.0).astype(BF16)
    pick_ref[...] = pick
    known = jnp.concatenate([xy_ref[...] * SCALE, jnp.zeros((6, NB), F32)], axis=0)
    at = dot(jnp.concatenate(split3(known), axis=0), pick)
    at = (at[16:] + at[8:16]) + at[:8]
    half = [at[:2, :R], at[:2, R:]]
    xy_at_ref[...] = jnp.concatenate([half[0][0:1], half[1][0:1], half[0][1:2], half[1][1:2], jnp.zeros((12, R), F32)], axis=0)


def near_kernel(recv_ref, xy_at_ref, near_ref, out_ref):
    me = lax.axis_index("x") * 2 + lax.axis_index("core")
    my_z = lax.axis_index("z")
    level = lax.broadcasted_iota(jnp.int32, (S, 512), 1) // R
    row = lax.broadcasted_iota(jnp.int32, (S, R), 0)
    total = jnp.zeros((S, 512), F32)
    extra = xy_at_ref[...]
    for q in range(XC):
        apart = me ^ q
        own_level = jnp.where(apart == 1, 0, jnp.where(apart < 4, 1, 2))
        own_level = jnp.where(apart == 0, -1, own_level)
        got = recv_ref[q]
        total = total + jnp.where((level == own_level) | (level >= 3), got, 0.0)
        extra = jnp.where(row == q + 8, got[:, LEVELS * R :], extra)
    near_ref[...] = total
    parts = [jnp.concatenate([total[:, (3 + k) * R : (4 + k) * R], extra], axis=1) for k in range(4)]
    for z in range(NZ):
        apart = my_z ^ z
        out_ref[z] = jnp.where(apart >= 8, parts[3], jnp.where(apart >= 4, parts[2], jnp.where(apart >= 2, parts[1], parts[0])))


def field_kernel(recv_ref, near_ref, local_ref, basis_ref, pick_ref, value_ref, field_ref, out_ref):
    my_z = lax.axis_index("z")
    far = [jnp.zeros((S, CAP), F32) for _ in range(4)]
    for z in range(NZ):
        apart = my_z ^ z
        got = recv_ref[z]
        for k in range(4):
            mine = (apart >= 2**k) & (apart < 2 ** (k + 1))
            far[k] = far[k] + jnp.where(mine, got, 0.0)
    coef = jnp.concatenate([near_ref[:, : 3 * R]] + [f[:, :R] for f in far], axis=1)
    level = lax.broadcasted_iota(jnp.int32, (S, LEVELS * R), 1) // R
    factor = jnp.zeros((S, LEVELS * R), F32)
    for k in range(LEVELS):
        factor = jnp.where(level == k, 0.5 / math.sqrt(R * NB * 2.0**k), factor)
    coef = coef * factor
    low = dot(jnp.concatenate(split3(coef), axis=0), basis_ref[...])
    field = local_ref[...] + ((low[2 * S :] + low[S : 2 * S]) + low[:S])
    field_ref[...] = field
    at = dot(jnp.concatenate(split3(field), axis=0), pick_ref[...])
    residual = value_ref[...] - ((at[2 * S :] + at[S : 2 * S]) + at[:S])
    for z in range(NZ):
        out_ref[z] = residual


def spread_kernel(recv_ref, extra_ref, out_ref):
    for x in range(4):
        for z in range(NZ):
            out_ref[x, S * z : S * (z + 1)] = recv_ref[z]
    for z in range(0, NZ, 4):
        rows = []
        for zz in range(z, z + 4):
            rows += [jnp.concatenate([extra_ref[zz, 2 * i : 2 * i + 1, R:], extra_ref[zz, 2 * i + 1 : 2 * i + 2, R:]], axis=1) for i in range(2)]
        rows = jnp.concatenate(rows, axis=0)
        for x in range(4):
            out_ref[x, S * NZ + 2 * z : S * NZ + 2 * z + 8] = rows


def join_kernel(own_hbm, next_ref, out_hbm, held, sems):
    arrived = pltpu.make_async_copy(next_ref, out_hbm.at[1], sems.at[1])
    arrived.start()
    fetch(sems, [(own_hbm, held)])
    fetch(sems, [(held, out_hbm.at[0])])
    arrived.wait()


def inverse_kernel(near_hbm, far_hbm, out_ref, held, sems):
    fetch(sems, [(ref.at[d], held.at[2 * i + d]) for i, ref in enumerate((near_hbm, far_hbm)) for d in range(2)])
    my_y = lax.axis_index("y")

    def one_part(j, carry):
        at = pl.multiple_of(j * 256, 256)
        got = [held[d, :, pl.ds(at, 256)] for d in range(4)]
        rows = []
        for y in range(4):
            apart = my_y ^ y
            rows.append(jnp.where(apart >= 2, jnp.where(apart == 2, got[2], got[3]), jnp.where(apart == 0, got[0], got[1])))
        rows = jnp.concatenate(rows, axis=0)
        hi = rows.astype(BF16).astype(F32)
        out_ref[pl.ds(at, 256)] = jnp.transpose(jnp.concatenate([hi, rows - hi], axis=0)).astype(BF16)
        return carry

    lax.fori_loop(0, M // 256, one_part, 0, unroll=4)


def pack(base_ref, count_ref, ref, c, packed, xy_ref):
    lane = lax.broadcasted_iota(jnp.int32, (S, CAP), 1)

    def one_column(x, carry):
        for z in range(NZ):
            p = 8 * z + 2 * x + c
            base, count = base_ref[p], count_ref[p]
            shift = base % CAP
            start = pl.multiple_of(base - shift, CAP)
            end = shift + count
            first = (lane >= shift) & (lane < end)
            second = lane < end - CAP
            got = pltpu.roll(ref[x, S * z : S * (z + 1)], shift, 1)
            pltpu.store(packed.at[:, pl.ds(start, CAP)], got, mask=first)
            pltpu.store(packed.at[:, pl.ds(start + CAP, CAP)], got, mask=second)
            got = pltpu.roll(ref[x, S * NZ + 2 * z : S * NZ + 2 * z + 2], shift, 1)
            pltpu.store(xy_ref.at[:, pl.ds(start, CAP)], got, mask=first[:2])
            pltpu.store(xy_ref.at[:, pl.ds(start + CAP, CAP)], got, mask=second[:2])
        return carry

    lax.fori_loop(0, 4, one_column, 0)


def pack_kernel(base_ref, count_ref, own_ref, packed, xy_ref):
    pack(base_ref, count_ref, own_ref, lax.axis_index("core"), packed, xy_ref)


def coef_kernel(base_ref, count_ref, other_ref, inv_ref, packed_in, xy_in, packed, xy_ref, out_ref):
    pack(base_ref, count_ref, other_ref, 1 - lax.axis_index("core"), packed, xy_ref)
    acc = jnp.zeros((2 * S, 2 * ROWS), F32)
    width = 1024
    for k in range(0, M, width):
        acc = acc + dot(jnp.concatenate(split2(packed[:, k : k + width]), axis=0), inv_ref[k : k + width])
    coef = acc[:S] + acc[S:]
    coef = coef[:, :ROWS] + coef[:, ROWS:]
    piece = jnp.concatenate([coef[: S // 2], coef[S // 2 :]], axis=1)
    for i in range(M // CAP):
        out_ref[i] = piece


HALF = M // 2
CHUNK = 256
KEPT = 12


def cross_kernel(obs_ref, xy_ref, kept_ref, own_hbm, other_hbm, buf, sems):
    core = lax.axis_index("core")
    sx = xy_ref[0:1] * SCALE
    sy = xy_ref[1:2] * SCALE

    def rows(i):
        return pl.ds(pl.multiple_of(i * CHUNK, CHUNK), CHUNK)

    def copies(i, slot, own_ref, first):
        return [
            pltpu.make_async_copy(buf.at[slot, 0], own_ref.at[rows(i - first)], sems.at[slot, 0]),
            pltpu.make_async_copy(buf.at[slot, 1], other_hbm.at[rows(i)], sems.at[slot, 1]),
        ]

    def step(own_ref, first):
        def run(i, carry):
            slot = i % 2

            @pl.when(i > 1)
            def _():
                for copy in copies(first, slot, own_ref, first):
                    copy.wait()

            for m in range(4):
                at = pl.multiple_of(2 * CHUNK * i + CAP * m, CAP)
                ox = jnp.transpose(jnp.broadcast_to(obs_ref[0:1, pl.ds(at, CAP)], (CAP, CAP)))
                oy = jnp.transpose(jnp.broadcast_to(obs_ref[1:2, pl.ds(at, CAP)], (CAP, CAP)))
                for h in range(0, NB, CAP):
                    dx = ox - sx[:, h : h + CAP]
                    dy = oy - sy[:, h : h + CAP]
                    square = jnp.maximum(dx * dx + dy * dy, 1e-30)
                    hi, lo = split2(jnp.exp2(-(square * lax.rsqrt(square))))
                    for c in range(2):
                        for part, left in ((hi, h), (lo, NB + h)):
                            buf[slot, core ^ c, ROWS * m : ROWS * (m + 1), left : left + CAP] = part[ROWS * c : ROWS * (c + 1)]
            for copy in copies(i, slot, own_ref, first):
                copy.start()
            return carry

        return run

    steps = HALF // CHUNK
    lax.fori_loop(0, KEPT, step(kept_ref, 0), 0)
    lax.fori_loop(KEPT, steps, step(own_hbm, KEPT), 0)
    for i in range(steps - 2, steps):
        for copy in copies(i, i % 2, own_hbm, KEPT):
            copy.wait()


def coef_chunk(pieces_ref, k):
    lane = lax.broadcasted_iota(jnp.int32, (S // 2, CAP), 1)
    blocks = []
    for m in range(4 * k, 4 * k + 4, 2):
        even, odd = pieces_ref[m], pieces_ref[m + 1]
        first = jnp.where(lane < ROWS, even, pltpu.roll(odd, ROWS, 1))
        second = jnp.where(lane < ROWS, pltpu.roll(even, ROWS, 1), odd)
        blocks.append(jnp.concatenate([first, second], axis=0))
    return jnp.concatenate(split2(jnp.concatenate(blocks, axis=1)), axis=0)


def fold(acc):
    acc = acc[:S] + acc[S:]
    return acc[:, :NB] + acc[:, NB:]


def own_half_kernel(pieces_ref, kept_ref, own_hbm, other_hbm, out_ref, other_ref, buf, sems, other_sem):
    steps = HALF // CHUNK
    rows = [pl.ds(i * CHUNK, CHUNK) for i in range(steps)]
    copies = [pltpu.make_async_copy(own_hbm.at[rows[i]], buf.at[i], sems.at[i]) for i in range(steps - KEPT)]
    others = [pltpu.make_async_copy(other_hbm.at[rows[i]], other_ref.at[rows[i]], other_sem.at[i]) for i in range(steps)]
    for copy in copies + others:
        copy.start()
    acc = jnp.zeros((2 * S, 2 * NB), F32)
    for k in range(steps):
        left = coef_chunk(pieces_ref, k)
        if k < KEPT:
            right = kept_ref[rows[k]]
        else:
            copies[k - KEPT].wait()
            right = buf[k - KEPT]
        acc = acc + dot(left, right)
    out_ref[...] = fold(acc)
    for copy in others:
        copy.wait()


def other_half_kernel(pieces_ref, tile_ref, partial_ref, field_ref, out_ref):
    acc = jnp.zeros((2 * S, 2 * NB), F32)
    for k in range(HALF // CHUNK):
        acc = acc + dot(coef_chunk(pieces_ref, k), tile_ref[k * CHUNK : (k + 1) * CHUNK])
    out_ref[...] = field_ref[...] + (partial_ref[...] + fold(acc))


def call(name, kernel, out, specs, scratch=(), flops=0, nbytes=0, out_specs=None, aliases=None):
    out_specs = out_specs or [VMEM] * len(out)
    shapes = [pltpu.MemorySpace.HBM(s, d) if spec is HBM else jax.ShapeDtypeStruct(s, d) for (s, d), spec in zip(out, out_specs)]
    made = pl.pallas_call(
        kernel,
        out_shape=shapes,
        in_specs=specs,
        out_specs=out_specs,
        scratch_shapes=list(scratch),
        input_output_aliases=aliases or {},
        compiler_params=pltpu.CompilerParams(vmem_limit_bytes=VMEM_MIB[name] << 20 if name in VMEM_MIB else None),
        cost_estimate=pl.CostEstimate(flops=flops, bytes_accessed=nbytes, transcendentals=0),
    )

    def run(*args):
        return made(*(pltpu.with_memory_space_constraint(a, pltpu.MemorySpace.HBM) if spec is HBM else a for a, spec in zip(args, specs)))

    return run


def exchange(piece, axes):
    return lax.all_to_all(piece, axes, 0, 0, tiled=True)


def body(samples_z, diag_block, level_basis, site_xy, obs_site, obs_value, obs_count, inverse_rows):
    basis = level_basis.reshape(LEVELS * R, NB)
    block = lax.ppermute(inverse_rows, "y", [(y, y ^ 1) for y in range(4)])
    (pair,) = call(
        "join",
        join_kernel,
        [((2, S, M), F32)],
        [HBM, VMEM],
        [pltpu.VMEM((S, M), F32), pltpu.SemaphoreType.DMA((2,))],
        out_specs=[HBM],
    )(inverse_rows, block)
    far_pair = lax.ppermute(pair, "y", [(y, y ^ 2) for y in range(4)])

    (piece,) = call("project", project_kernel, [((XC, S, 512), F32)], [VMEM, VMEM, SMEM])(samples_z, basis, obs_count)
    recv = exchange(piece, ("x", "core"))
    local, pick, xy_at, xy, basis, value = call(
        "local",
        local_kernel,
        [((S, NB), F32), ((NB, CAP), BF16), ((S, R), F32), ((2, NB), F32), ((LEVELS * R, NB), BF16), ((1, CAP), F32)],
        [HBM] * 6,
        [pltpu.VMEM((NB, NB), BF16), pltpu.VMEM((1, CAP), jnp.int32), pltpu.VMEM((S, NB), BF16), pltpu.SemaphoreType.DMA((6,))],
        flops=2 * S * NB * NB,
        nbytes=1 << 18,
    )(samples_z, diag_block, site_xy, obs_site.reshape(1, CAP), basis, obs_value.reshape(1, CAP))
    near, piece = call("near", near_kernel, [((S, 512), F32), ((NZ, S, CAP), F32)], [VMEM] * 2)(recv, xy_at)
    extra = exchange(piece, "z")
    counts = extra[:, 8:, R].reshape(XC * NZ)
    order = jnp.arange(XC * NZ, dtype=jnp.int32)
    base = jnp.sum(jnp.where(order[None, :] < order[:, None], counts[None, :], 0.0), axis=1).astype(jnp.int32)
    counts = counts.astype(jnp.int32)
    field, piece = call("field", field_kernel, [((S, NB), F32), ((NZ, S, CAP), F32)], [VMEM] * 6)(
        extra, near, local, basis, pick, value
    )
    (inv,) = call(
        "inverse",
        inverse_kernel,
        [((M, 2 * ROWS), BF16)],
        [HBM] * 2,
        [pltpu.VMEM((4, S, M), F32), pltpu.SemaphoreType.DMA((4,))],
        flops=20 * ROWS * M,
        nbytes=8 * ROWS * M,
    )(pair, far_pair)
    recv = exchange(piece, "z")
    (piece,) = call("spread", spread_kernel, [((4, 18 * NZ, CAP), F32)], [VMEM] * 2)(recv, extra)
    own = exchange(piece, "x")
    other = lax.ppermute(own, "core", [(0, 1), (1, 0)])
    width = M + 2 * CAP
    packed, obs_xy = call("pack", pack_kernel, [((S, width), F32), ((2, width), F32)], [SMEM, SMEM, VMEM])(base, counts, own)
    _, obs_xy, piece = call(
        "coef",
        coef_kernel,
        [((S, width), F32), ((2, width), F32), ((M // CAP, S // 2, CAP), F32)],
        [SMEM, SMEM] + [VMEM] * 4,
        flops=4 * 2 * S * ROWS * M,
        nbytes=4 * ROWS * M,
        aliases={4: 0, 5: 1},
    )(base, counts, other, inv, packed, obs_xy)
    kept, own_tile, other_tile = call(
        "cross",
        cross_kernel,
        [((KEPT * CHUNK, 2 * NB), BF16), ((HALF - KEPT * CHUNK, 2 * NB), BF16), ((HALF, 2 * NB), BF16)],
        [VMEM, VMEM],
        [pltpu.VMEM((2, 2, CHUNK, 2 * NB), BF16), pltpu.SemaphoreType.DMA((2, 2))],
        flops=20 * NB * M,
        nbytes=4 * NB * M,
        out_specs=[VMEM, HBM, HBM],
    )(obs_xy, xy)
    own = exchange(piece, ("z", "x"))
    other = lax.ppermute(own, "core", [(0, 1), (1, 0)])
    streamed = HALF // CHUNK - KEPT
    partial, other_tile = call(
        "own_half",
        own_half_kernel,
        [((S, NB), F32), ((HALF, 2 * NB), BF16)],
        [VMEM, VMEM, HBM, HBM],
        [
            pltpu.VMEM((streamed, CHUNK, 2 * NB), BF16),
            pltpu.SemaphoreType.DMA((streamed,)),
            pltpu.SemaphoreType.DMA((HALF // CHUNK,)),
        ],
        flops=2 * 2 * S * NB * M,
        nbytes=4 * NB * M,
    )(own, kept, own_tile, other_tile)
    return call("other_half", other_half_kernel, [((S, NB), F32)], [VMEM] * 4, flops=2 * 2 * S * NB * M, nbytes=2 * NB * M)(
        other, other_tile, partial, field
    )[0]


def solution(mesh):
    grid = Mesh(mesh.devices.reshape(NZ, 4, 2, 4), ("z", "x", "core", "y"))
    leaf = ("z", "x", "core")
    in_specs = (
        P("y", leaf),
        P(leaf, None),
        P(None, None, leaf),
        P(None, leaf),
        P(leaf),
        P(leaf),
        P(leaf),
        P(("z", "x", "core", "y"), None),
    )

    return jax.shard_map(body, mesh=grid, in_specs=in_specs, out_specs=P("y", leaf), check_vma=False)
```

```python
import math

import jax
import jax.numpy as jnp
from jax import lax
from jax.experimental import pallas as pl
from jax.experimental.pallas import tpu as pltpu
from jax.sharding import Mesh, PartitionSpec as P


corr_length = 0.15
SCALE = math.log2(math.e) / corr_length
LEVELS = 7
R = 64
XC = 8
NZ = 16
S = 16
NB = 256
CAP = 128
M = 8192
ROWS = 64
F32 = jnp.float32
BF16 = jnp.bfloat16

VMEM = pl.BlockSpec(memory_space=pltpu.VMEM)
HBM = pl.BlockSpec(memory_space=pltpu.MemorySpace.HBM)
SMEM = pl.BlockSpec(memory_space=pltpu.SMEM)
NT = (((1,), (1,)), ((), ()))

VMEM_MIB = {'local': 2, 'near': 2, 'field': 4, 'inverse': 10, 'join': 4, 'spread': 4, 'pack': 4, 'coef': 10, 'cross': 8, 'own_half': 14, 'other_half': 10}


def dot(a, b, dims=(((1,), (0,)), ((), ()))):
    return lax.dot_general(a, b, dims, preferred_element_type=F32)


def split2(v):
    hi = v.astype(BF16)
    return hi, (v - hi.astype(F32)).astype(BF16)


def split3(v):
    hi = v.astype(BF16)
    rest = v - hi.astype(F32)
    mid = rest.astype(BF16)
    return hi, mid, (rest - mid.astype(F32)).astype(BF16)


def fetch(sems, pairs):
    copies = [pltpu.make_async_copy(src, dst, sems.at[i]) for i, (src, dst) in enumerate(pairs)]
    for copy in copies:
        copy.start()
    for copy in copies:
        copy.wait()


def project_kernel(z_ref, basis_ref, count_ref, out_ref):
    proj = dot(z_ref[...], basis_ref[...], NT)
    count = jnp.full((S, R), count_ref[0], jnp.int32).astype(F32)
    piece = jnp.concatenate([proj, count], axis=1)
    for q in range(XC):
        out_ref[q] = piece


def local_kernel(
    z_hbm, diag_hbm, xy_hbm, site_hbm, basis_hbm, value_hbm, field_ref, pick_ref, xy_at_ref, xy_ref, basis_ref, value_ref, diag_ref, site_ref, z_ref, sems
):
    fetch(sems, [(diag_hbm, diag_ref), (xy_hbm, xy_ref), (site_hbm, site_ref), (basis_hbm, basis_ref), (value_hbm, value_ref), (z_hbm, z_ref)])
    field_ref[...] = dot(z_ref[...], diag_ref[...])
    site = lax.broadcasted_iota(jnp.int32, (NB, CAP), 0)
    pick = jnp.where(site == site_ref[...], 1.0, 0.0).astype(BF16)
    pick_ref[...] = pick
    known = jnp.concatenate([xy_ref[...] * SCALE, jnp.zeros((6, NB), F32)], axis=0)
    at = dot(jnp.concatenate(split3(known), axis=0), pick)
    at = (at[16:] + at[8:16]) + at[:8]
    half = [at[:2, :R], at[:2, R:]]
    xy_at_ref[...] = jnp.concatenate([half[0][0:1], half[1][0:1], half[0][1:2], half[1][1:2], jnp.zeros((12, R), F32)], axis=0)


def near_kernel(recv_ref, xy_at_ref, near_ref, out_ref):
    me = lax.axis_index("x") * 2 + lax.axis_index("core")
    my_z = lax.axis_index("z")
    level = lax.broadcasted_iota(jnp.int32, (S, 512), 1) // R
    row = lax.broadcasted_iota(jnp.int32, (S, R), 0)
    total = jnp.zeros((S, 512), F32)
    extra = xy_at_ref[...]
    for q in range(XC):
        apart = me ^ q
        own_level = jnp.where(apart == 1, 0, jnp.where(apart < 4, 1, 2))
        own_level = jnp.where(apart == 0, -1, own_level)
        got = recv_ref[q]
        total = total + jnp.where((level == own_level) | (level >= 3), got, 0.0)
        extra = jnp.where(row == q + 8, got[:, LEVELS * R :], extra)
    near_ref[...] = total
    parts = [jnp.concatenate([total[:, (3 + k) * R : (4 + k) * R], extra], axis=1) for k in range(4)]
    for z in range(NZ):
        apart = my_z ^ z
        out_ref[z] = jnp.where(apart >= 8, parts[3], jnp.where(apart >= 4, parts[2], jnp.where(apart >= 2, parts[1], parts[0])))


def field_kernel(recv_ref, near_ref, local_ref, basis_ref, pick_ref, value_ref, field_ref, out_ref):
    my_z = lax.axis_index("z")
    far = [jnp.zeros((S, CAP), F32) for _ in range(4)]
    for z in range(NZ):
        apart = my_z ^ z
        got = recv_ref[z]
        for k in range(4):
            mine = (apart >= 2**k) & (apart < 2 ** (k + 1))
            far[k] = far[k] + jnp.where(mine, got, 0.0)
    coef = jnp.concatenate([near_ref[:, : 3 * R]] + [f[:, :R] for f in far], axis=1)
    level = lax.broadcasted_iota(jnp.int32, (S, LEVELS * R), 1) // R
    factor = jnp.zeros((S, LEVELS * R), F32)
    for k in range(LEVELS):
        factor = jnp.where(level == k, 0.5 / math.sqrt(R * NB * 2.0**k), factor)
    coef = coef * factor
    low = dot(jnp.concatenate(split3(coef), axis=0), basis_ref[...])
    field = local_ref[...] + ((low[2 * S :] + low[S : 2 * S]) + low[:S])
    field_ref[...] = field
    at = dot(jnp.concatenate(split3(field), axis=0), pick_ref[...])
    residual = value_ref[...] - ((at[2 * S :] + at[S : 2 * S]) + at[:S])
    for z in range(NZ):
        out_ref[z] = residual


def spread_kernel(recv_ref, extra_ref, out_ref):
    for x in range(4):
        for z in range(NZ):
            out_ref[x, S * z : S * (z + 1)] = recv_ref[z]
    for z in range(0, NZ, 4):
        rows = []
        for zz in range(z, z + 4):
            rows += [jnp.concatenate([extra_ref[zz, 2 * i : 2 * i + 1, R:], extra_ref[zz, 2 * i + 1 : 2 * i + 2, R:]], axis=1) for i in range(2)]
        rows = jnp.concatenate(rows, axis=0)
        for x in range(4):
            out_ref[x, S * NZ + 2 * z : S * NZ + 2 * z + 8] = rows


def join_kernel(own_hbm, next_ref, out_hbm, held, sems):
    arrived = pltpu.make_async_copy(next_ref, out_hbm.at[1], sems.at[1])
    arrived.start()
    fetch(sems, [(own_hbm, held)])
    fetch(sems, [(held, out_hbm.at[0])])
    arrived.wait()


def inverse_kernel(near_hbm, far_hbm, out_ref, held, sems):
    fetch(sems, [(ref.at[d], held.at[2 * i + d]) for i, ref in enumerate((near_hbm, far_hbm)) for d in range(2)])
    my_y = lax.axis_index("y")

    def one_part(j, carry):
        at = pl.multiple_of(j * 256, 256)
        got = [held[d, :, pl.ds(at, 256)] for d in range(4)]
        rows = []
        for y in range(4):
            apart = my_y ^ y
            rows.append(jnp.where(apart >= 2, jnp.where(apart == 2, got[2], got[3]), jnp.where(apart == 0, got[0], got[1])))
        rows = jnp.concatenate(rows, axis=0)
        hi = rows.astype(BF16).astype(F32)
        out_ref[pl.ds(at, 256)] = jnp.transpose(jnp.concatenate([hi, rows - hi], axis=0)).astype(BF16)
        return carry

    lax.fori_loop(0, M // 256, one_part, 0, unroll=4)


def pack(base_ref, count_ref, ref, c, packed, xy_ref):
    lane = lax.broadcasted_iota(jnp.int32, (S, CAP), 1)

    def one_column(x, carry):
        for z in range(NZ):
            p = 8 * z + 2 * x + c
            base, count = base_ref[p], count_ref[p]
            shift = base % CAP
            start = pl.multiple_of(base - shift, CAP)
            end = shift + count
            first = (lane >= shift) & (lane < end)
            second = lane < end - CAP
            got = pltpu.roll(ref[x, S * z : S * (z + 1)], shift, 1)
            pltpu.store(packed.at[:, pl.ds(start, CAP)], got, mask=first)
            pltpu.store(packed.at[:, pl.ds(start + CAP, CAP)], got, mask=second)
            got = pltpu.roll(ref[x, S * NZ + 2 * z : S * NZ + 2 * z + 2], shift, 1)
            pltpu.store(xy_ref.at[:, pl.ds(start, CAP)], got, mask=first[:2])
            pltpu.store(xy_ref.at[:, pl.ds(start + CAP, CAP)], got, mask=second[:2])
        return carry

    lax.fori_loop(0, 4, one_column, 0)


def pack_kernel(base_ref, count_ref, own_ref, packed, xy_ref):
    pack(base_ref, count_ref, own_ref, lax.axis_index("core"), packed, xy_ref)


def coef_kernel(base_ref, count_ref, other_ref, inv_ref, packed_in, xy_in, packed, xy_ref, out_ref):
    pack(base_ref, count_ref, other_ref, 1 - lax.axis_index("core"), packed, xy_ref)
    acc = jnp.zeros((2 * S, 2 * ROWS), F32)
    width = 1024
    for k in range(0, M, width):
        acc = acc + dot(jnp.concatenate(split2(packed[:, k : k + width]), axis=0), inv_ref[k : k + width])
    coef = acc[:S] + acc[S:]
    coef = coef[:, :ROWS] + coef[:, ROWS:]
    piece = jnp.concatenate([coef[: S // 2], coef[S // 2 :]], axis=1)
    for i in range(M // CAP):
        out_ref[i] = piece


HALF = M // 2
CHUNK = 256
KEPT = 12


def cross_kernel(obs_ref, xy_ref, kept_ref, own_hbm, other_hbm, buf, sems):
    core = lax.axis_index("core")
    sx = xy_ref[0:1] * SCALE
    sy = xy_ref[1:2] * SCALE

    def rows(i):
        return pl.ds(pl.multiple_of(i * CHUNK, CHUNK), CHUNK)

    def copies(i, slot, own_ref, first):
        return [
            pltpu.make_async_copy(buf.at[slot, 0], own_ref.at[rows(i - first)], sems.at[slot, 0]),
            pltpu.make_async_copy(buf.at[slot, 1], other_hbm.at[rows(i)], sems.at[slot, 1]),
        ]

    def step(own_ref, first):
        def run(i, carry):
            slot = i % 2

            @pl.when(i > 1)
            def _():
                for copy in copies(first, slot, own_ref, first):
                    copy.wait()

            for m in range(4):
                at = pl.multiple_of(2 * CHUNK * i + CAP * m, CAP)
                ox = jnp.transpose(jnp.broadcast_to(obs_ref[0:1, pl.ds(at, CAP)], (CAP, CAP)))
                oy = jnp.transpose(jnp.broadcast_to(obs_ref[1:2, pl.ds(at, CAP)], (CAP, CAP)))
                for h in range(0, NB, CAP):
                    dx = ox - sx[:, h : h + CAP]
                    dy = oy - sy[:, h : h + CAP]
                    square = jnp.maximum(dx * dx + dy * dy, 1e-30)
                    hi, lo = split2(jnp.exp2(-(square * lax.rsqrt(square))))
                    for c in range(2):
                        for part, left in ((hi, h), (lo, NB + h)):
                            buf[slot, core ^ c, ROWS * m : ROWS * (m + 1), left : left + CAP] = part[ROWS * c : ROWS * (c + 1)]
            for copy in copies(i, slot, own_ref, first):
                copy.start()
            return carry

        return run

    steps = HALF // CHUNK
    lax.fori_loop(0, KEPT, step(kept_ref, 0), 0)
    lax.fori_loop(KEPT, steps, step(own_hbm, KEPT), 0)
    for i in range(steps - 2, steps):
        for copy in copies(i, i % 2, own_hbm, KEPT):
            copy.wait()


AHEAD = 8


def coef_chunk(pieces_ref, k):
    lane = lax.broadcasted_iota(jnp.int32, (S // 2, CAP), 1)
    blocks = []
    for m in range(4 * k, 4 * k + 4, 2):
        even, odd = pieces_ref[m], pieces_ref[m + 1]
        first = jnp.where(lane < ROWS, even, pltpu.roll(odd, ROWS, 1))
        second = jnp.where(lane < ROWS, pltpu.roll(even, ROWS, 1), odd)
        blocks.append(jnp.concatenate([first, second], axis=0))
    return jnp.concatenate(split2(jnp.concatenate(blocks, axis=1)), axis=0)


def chunk_copies(tile_hbm, chunks, ref, sems):
    copies = [
        pltpu.make_async_copy(tile_hbm.at[pl.ds(k * CHUNK, CHUNK)], ref.at[pl.ds(i * CHUNK, CHUNK)], sems.at[i])
        for i, k in enumerate(chunks)
    ]
    for copy in copies:
        copy.start()
    return copies


def half_product(pieces_ref, kept_ref, buf, copies):
    kept = HALF // CHUNK - len(copies)
    acc = jnp.zeros((2 * S, 2 * NB), F32)
    for k in range(HALF // CHUNK):
        left = coef_chunk(pieces_ref, k)
        if k < kept:
            right = kept_ref[k * CHUNK : (k + 1) * CHUNK]
        else:
            copies[k - kept].wait()
            right = buf[(k - kept) * CHUNK : (k - kept + 1) * CHUNK]
        acc = acc + dot(left, right)
    acc = acc[:S] + acc[S:]
    return acc[:, :NB] + acc[:, NB:]


def own_half_kernel(pieces_ref, kept_ref, own_hbm, other_hbm, out_ref, ahead_ref, buf, sems, ahead_sems):
    copies = chunk_copies(own_hbm, range(HALF // CHUNK - KEPT), buf, sems)
    ahead = chunk_copies(other_hbm, range(AHEAD), ahead_ref, ahead_sems)
    out_ref[...] = half_product(pieces_ref, kept_ref, buf, copies)
    for copy in ahead:
        copy.wait()


def other_half_kernel(pieces_ref, ahead_ref, other_hbm, partial_ref, field_ref, out_ref, buf, sems):
    copies = chunk_copies(other_hbm, range(AHEAD, HALF // CHUNK), buf, sems)
    out_ref[...] = field_ref[...] + (partial_ref[...] + half_product(pieces_ref, ahead_ref, buf, copies))


def call(name, kernel, out, specs, scratch=(), flops=0, nbytes=0, out_specs=None, aliases=None):
    out_specs = out_specs or [VMEM] * len(out)
    shapes = [pltpu.MemorySpace.HBM(s, d) if spec is HBM else jax.ShapeDtypeStruct(s, d) for (s, d), spec in zip(out, out_specs)]
    made = pl.pallas_call(
        kernel,
        out_shape=shapes,
        in_specs=specs,
        out_specs=out_specs,
        scratch_shapes=list(scratch),
        input_output_aliases=aliases or {},
        compiler_params=pltpu.CompilerParams(vmem_limit_bytes=VMEM_MIB[name] << 20 if name in VMEM_MIB else None),
        cost_estimate=pl.CostEstimate(flops=flops, bytes_accessed=nbytes, transcendentals=0),
    )

    def run(*args):
        return made(*(pltpu.with_memory_space_constraint(a, pltpu.MemorySpace.HBM) if spec is HBM else a for a, spec in zip(args, specs)))

    return run


def exchange(piece, axes):
    return lax.all_to_all(piece, axes, 0, 0, tiled=True)


def body(samples_z, diag_block, level_basis, site_xy, obs_site, obs_value, obs_count, inverse_rows):
    basis = level_basis.reshape(LEVELS * R, NB)
    block = lax.ppermute(inverse_rows, "y", [(y, y ^ 1) for y in range(4)])
    (pair,) = call(
        "join",
        join_kernel,
        [((2, S, M), F32)],
        [HBM, VMEM],
        [pltpu.VMEM((S, M), F32), pltpu.SemaphoreType.DMA((2,))],
        out_specs=[HBM],
    )(inverse_rows, block)
    far_pair = lax.ppermute(pair, "y", [(y, y ^ 2) for y in range(4)])

    (piece,) = call("project", project_kernel, [((XC, S, 512), F32)], [VMEM, VMEM, SMEM])(samples_z, basis, obs_count)
    recv = exchange(piece, ("x", "core"))
    local, pick, xy_at, xy, basis, value = call(
        "local",
        local_kernel,
        [((S, NB), F32), ((NB, CAP), BF16), ((S, R), F32), ((2, NB), F32), ((LEVELS * R, NB), BF16), ((1, CAP), F32)],
        [HBM] * 6,
        [pltpu.VMEM((NB, NB), BF16), pltpu.VMEM((1, CAP), jnp.int32), pltpu.VMEM((S, NB), BF16), pltpu.SemaphoreType.DMA((6,))],
        flops=2 * S * NB * NB,
        nbytes=1 << 18,
    )(samples_z, diag_block, site_xy, obs_site.reshape(1, CAP), basis, obs_value.reshape(1, CAP))
    near, piece = call("near", near_kernel, [((S, 512), F32), ((NZ, S, CAP), F32)], [VMEM] * 2)(recv, xy_at)
    extra = exchange(piece, "z")
    counts = extra[:, 8:, R].reshape(XC * NZ)
    order = jnp.arange(XC * NZ, dtype=jnp.int32)
    base = jnp.sum(jnp.where(order[None, :] < order[:, None], counts[None, :], 0.0), axis=1).astype(jnp.int32)
    counts = counts.astype(jnp.int32)
    field, piece = call("field", field_kernel, [((S, NB), F32), ((NZ, S, CAP), F32)], [VMEM] * 6)(
        extra, near, local, basis, pick, value
    )
    (inv,) = call(
        "inverse",
        inverse_kernel,
        [((M, 2 * ROWS), BF16)],
        [HBM] * 2,
        [pltpu.VMEM((4, S, M), F32), pltpu.SemaphoreType.DMA((4,))],
        flops=20 * ROWS * M,
        nbytes=8 * ROWS * M,
    )(pair, far_pair)
    recv = exchange(piece, "z")
    (piece,) = call("spread", spread_kernel, [((4, 18 * NZ, CAP), F32)], [VMEM] * 2)(recv, extra)
    own = exchange(piece, "x")
    other = lax.ppermute(own, "core", [(0, 1), (1, 0)])
    width = M + 2 * CAP
    packed, obs_xy = call("pack", pack_kernel, [((S, width), F32), ((2, width), F32)], [SMEM, SMEM, VMEM])(base, counts, own)
    _, obs_xy, piece = call(
        "coef",
        coef_kernel,
        [((S, width), F32), ((2, width), F32), ((M // CAP, S // 2, CAP), F32)],
        [SMEM, SMEM] + [VMEM] * 4,
        flops=4 * 2 * S * ROWS * M,
        nbytes=4 * ROWS * M,
        aliases={4: 0, 5: 1},
    )(base, counts, other, inv, packed, obs_xy)
    kept, own_tile, other_tile = call(
        "cross",
        cross_kernel,
        [((KEPT * CHUNK, 2 * NB), BF16), ((HALF - KEPT * CHUNK, 2 * NB), BF16), ((HALF, 2 * NB), BF16)],
        [VMEM, VMEM],
        [pltpu.VMEM((2, 2, CHUNK, 2 * NB), BF16), pltpu.SemaphoreType.DMA((2, 2))],
        flops=20 * NB * M,
        nbytes=4 * NB * M,
        out_specs=[VMEM, HBM, HBM],
    )(obs_xy, xy)
    own = exchange(piece, ("z", "x"))
    other = lax.ppermute(own, "core", [(0, 1), (1, 0)])
    streamed, late = HALF // CHUNK - KEPT, HALF // CHUNK - AHEAD
    partial, ahead = call(
        "own_half",
        own_half_kernel,
        [((S, NB), F32), ((AHEAD * CHUNK, 2 * NB), BF16)],
        [VMEM, VMEM, HBM, HBM],
        [
            pltpu.VMEM((streamed * CHUNK, 2 * NB), BF16),
            pltpu.SemaphoreType.DMA((streamed,)),
            pltpu.SemaphoreType.DMA((AHEAD,)),
        ],
        flops=2 * 2 * S * NB * M,
        nbytes=4 * NB * M,
    )(own, kept, own_tile, other_tile)
    return call(
        "other_half",
        other_half_kernel,
        [((S, NB), F32)],
        [VMEM, VMEM, HBM, VMEM, VMEM],
        [pltpu.VMEM((late * CHUNK, 2 * NB), BF16), pltpu.SemaphoreType.DMA((late,))],
        flops=2 * 2 * S * NB * M,
        nbytes=2 * NB * M,
    )(other, ahead, other_tile, partial, field)[0]


def solution(mesh):
    grid = Mesh(mesh.devices.reshape(NZ, 4, 2, 4), ("z", "x", "core", "y"))
    leaf = ("z", "x", "core")
    in_specs = (
        P("y", leaf),
        P(leaf, None),
        P(None, None, leaf),
        P(None, leaf),
        P(leaf),
        P(leaf),
        P(leaf),
        P(("z", "x", "core", "y"), None),
    )

    return jax.shard_map(body, mesh=grid, in_specs=in_specs, out_specs=P("y", leaf), check_vma=False)
```
